512 devices in a mesh: dp: 32 (over y, x, core), mp: 16 (over z).
Axes of the slice: x: 4, y: 4, z: 16, core: 2. Of those that a mesh axis runs over, the one named last changes fastest.
Arguments:
- task_codes: bfloat16 [64, 128], replicated, may hold values from -6 to 6
- hyper_weight: bfloat16 [128, 196608], P(None, ('dp', 'mp')), may hold values from -0.5 to 0.5
- frozen_weight: bfloat16 [5120, 1024], P('mp'), may hold values from -0.125 to 0.125
- tokens: bfloat16 [131072, 5120], P(('dp', 'mp')), may hold values from -6 to 6
- teacher: bfloat16 [131072, 1024], P(('dp', 'mp')), may hold values from -6 to 6
- seq_slot: int32 [1024], P(('dp', 'mp')), may hold values from 0 to 3, as said below
- task_share: int32 [32], replicated, may hold values from 1 to 4, as said below
- token_counts: int32 [64], replicated, may hold values from 1024 to 3071
Outputs:
- hyper_grad: float32 [128, 196608], P(None, ('dp', 'mp'))
The draws below stay inside these ranges and needn't reach their ends.
Inputs may be any that keep to these rules, and one draw needn't show every extreme that they name: Group g owns task_share[g] tasks, numbered after those of groups 0 to g - 1; the entries sum to 64; in every draw some group owns exactly 4 tasks. For sequence s of group g = s // 32, seq_slot[s] < task_share[g]; in every group some sequence names the group's last task.
All inputs are finite; a program needn't handle non-finite values.
Results may differ from the reference program's by a relative error of at most 0.012.
Values may be sent and summed in bfloat16 or wider, within the bound.
A program may use at most 64 MiB of HBM per device.

```python
import math
import jax
import jax.numpy as jnp
from jax import lax

D = 5120
KV = 1024
R = 32
H = 128
TASK_GRP = 2
TPG = 4
TOK_DEV = 256
SEQ_LEN = 128
TASKS = 64
TOK_GRP = 4096
TOKENS = 131072
SEQ_GRP = 32
SEQS = 1024
P_SIZE = 196608
N_DP = 32
N_MP = 16


def fraction_lookup(key):
    groups = TASKS // TASK_GRP
    base_key = jax.random.fold_in(key, 7)
    ordering = jax.random.permutation(jax.random.fold_in(base_key, 1), groups)
    heaviest = ordering[0]
    tallies = jnp.full((groups,), TASK_GRP, jnp.int32).at[heaviest].set(TPG)

    def lower_one(position, carried):
        current, remain = carried
        target = ordering[position]
        amount = jnp.minimum(remain, TASK_GRP - 1).astype(jnp.int32)
        return (current.at[target].add(-amount), remain - amount)
    tallies, remain = lax.fori_loop(1, groups, lower_one, (tallies, jnp.int32(TPG - TASK_GRP)))

    def move_one(step_index, current):
        step_key = jax.random.fold_in(base_key, 100 + step_index)
        source = jax.random.randint(jax.random.fold_in(step_key, 1), (), 0, groups, dtype=jnp.int32)
        destination = jax.random.randint(jax.random.fold_in(step_key, 2), (), 0, groups, dtype=jnp.int32)
        allowed = (current[source] > 1) & (current[destination] < TPG) & (source != heaviest) & (source != destination)
        change = allowed.astype(jnp.int32)
        return current.at[source].add(-change).at[destination].add(change)
    return lax.fori_loop(0, 4 * groups, move_one, tallies)


def draw_task_share(key, part):
    return fraction_lookup(key).astype(jnp.int32)


def draw_seq_slot(key, part):
    tallies = fraction_lookup(key)
    groups = TASKS // TASK_GRP
    owners = jnp.arange(SEQS, dtype=jnp.int32) // SEQ_GRP
    limits = tallies[owners]
    raw_bits = jax.random.randint(jax.random.fold_in(key, 11), (SEQS,), 0, 1 << 20, dtype=jnp.int32)
    slot_draw = raw_bits % limits
    marked = jax.random.randint(jax.random.fold_in(key, 13), (groups,), 0, SEQ_GRP, dtype=jnp.int32)
    is_marked = jnp.arange(SEQS, dtype=jnp.int32) % SEQ_GRP == marked[owners]
    return jnp.where(is_marked, limits - 1, slot_draw).astype(jnp.int32)


def plant(result, own_key, low, top_value):
    longest = result.shape.index(max(result.shape))
    spots = []
    for shift in (0, 1):
        where = [jax.random.randint(jax.random.fold_in(own_key, axis), (), 0, length) for axis, length in enumerate(result.shape)]
        where[longest] = (where[longest] + shift) % result.shape[longest]
        spots.append(tuple(where))
    return result.at[spots[0]].set(low).at[spots[1]].set(top_value)


def raised(values, own_key, source, target, shards_of, factor):
    def block_of(axis_at):
        return (jnp.arange(values.shape[axis_at]) // (values.shape[axis_at] // shards_of)).reshape((-1,) + (1,) * (values.ndim - 1 - axis_at))

    first = jax.random.permutation(own_key, shards_of)[block_of(target)]
    far = (block_of(target) + shards_of // 2) % shards_of
    return jnp.where((block_of(source) == first) | (block_of(source) == far), factor * values, values)


def steps_of(rng, dims, pieces, least, largest):
    level = 1.0
    for axis_at, blocks in pieces:
        draws = jax.random.uniform(jax.random.fold_in(jax.random.fold_in(rng, 6), axis_at), (blocks,), jnp.float32, least / len(pieces), largest / len(pieces))
        level = level * jnp.repeat(jnp.exp(draws), dims[axis_at] // blocks).reshape((-1,) + (1,) * (len(dims) - 1 - axis_at))
    return level


def noise(rng, extent, deviation, limit, shards=(), held_as=jnp.bfloat16):
    gain = steps_of(rng, extent, shards, -0.22, 0.18) if shards else 1.0
    result = jax.random.normal(rng, extent, jnp.float32) * deviation * gain
    return jnp.minimum(jnp.maximum(result, -limit), limit).astype(held_as)


def heavy_noise(rng, dims, width, bound, cuts, heavy, kind=jnp.bfloat16):
    entries = width * jax.random.normal(rng, dims, jnp.float32)
    if cuts:
        entries = entries * steps_of(rng, dims, cuts, -0.22, 0.18)
    return jnp.clip(raised(entries, jax.random.fold_in(rng, 3), *heavy), -bound, bound).astype(kind)


def setup_inputs(seed: int = 0) -> dict:
    key_list = jax.random.split(jax.random.key(seed), 9)
    return {
        "task_codes": noise(key_list[0], (TASKS, H), 1.0, 6.0),
        "hyper_weight": noise(key_list[1], (H, P_SIZE), H ** -0.5, 0.5, ((1, 512),)),
        "frozen_weight": heavy_noise(key_list[2], (D, KV), D ** -0.5, 0.125, ((0, 16),), (0, 1, 16, 2.0)),
        "tokens": noise(key_list[3], (TOKENS, D), 1.0, 6.0, ((0, 512),)),
        "teacher": noise(key_list[4], (TOKENS, KV), 1.0, 6.0, ((0, 512),)),
        "seq_slot": draw_seq_slot(jax.random.fold_in(key_list[8], 71), 0),
        "task_share": draw_task_share(jax.random.fold_in(key_list[8], 71), 0),
        "token_counts": plant(jax.random.randint(key_list[7], (TASKS,), 1024, 3072), jax.random.fold_in(key_list[7], 1), 1024, 3071).astype(jnp.int32),
    }


def reference(task_codes, hyper_weight, frozen_weight, tokens, teacher, seq_slot, task_share, token_counts):
    adapters = jnp.dot(task_codes, hyper_weight, preferred_element_type=jnp.float32).astype(jnp.bfloat16)
    offsets = (jnp.cumsum(task_share) - task_share).astype(jnp.int32)
    group_of = (jnp.arange(SEQS, dtype=jnp.int32) // SEQ_GRP).astype(jnp.int32)
    seq_task = (offsets[group_of] + seq_slot).astype(jnp.int32)
    counts = token_counts.astype(jnp.float32)
    task_weight = jnp.mean(counts) / counts
    shrink_factor = 1.0 / math.sqrt(D)
    rank_scale = 1.0 / math.sqrt(R)
    loss_scale = 1.0 / math.sqrt(TOK_GRP)
    seq_dev = TOK_DEV // SEQ_LEN
    blocks_all = N_DP * N_MP
    token_blocks = tokens.reshape(blocks_all, seq_dev, SEQ_LEN, D)
    teacher_blocks = teacher.reshape(blocks_all, seq_dev, SEQ_LEN, KV)
    blocks_per_task = seq_task.reshape(blocks_all, seq_dev)
    earlier = jnp.tril(jnp.ones((seq_dev, seq_dev), jnp.float32), -1)

    def one_block(accumulated, inputs):
        tokens_per_block, block_teacher, block_tasks = inputs
        chosen = jnp.take(adapters, block_tasks, axis=0).astype(jnp.float32)
        adapter_input = chosen[:, :D * R].reshape(seq_dev, D, R)
        adapter_out = chosen[:, D * R:].reshape(seq_dev, R, KV)
        flat_tokens = tokens_per_block.reshape(TOK_DEV, D)
        wide_sample_matrix = tokens_per_block.astype(jnp.float32)
        compact_factor_carry = lax.optimization_barrier((jnp.einsum('uep,upm->uem', wide_sample_matrix, adapter_input) * shrink_factor).astype(jnp.bfloat16))
        frozen_out = jnp.dot(flat_tokens, frozen_weight, preferred_element_type=jnp.float32).reshape(seq_dev, SEQ_LEN, KV)
        wide_low = compact_factor_carry.astype(jnp.float32)
        adapter_term = jnp.einsum('slr,srk->slk', wide_low, adapter_out) * rank_scale
        values = frozen_out + adapter_term
        weight = task_weight[block_tasks] * loss_scale
        value_grad = lax.optimization_barrier(((values - block_teacher.astype(jnp.float32)) * weight[:, None, None]).astype(jnp.bfloat16))
        expanded_derivative = value_grad.astype(jnp.float32)
        narrow_derivative = lax.optimization_barrier((jnp.einsum('slk,srk->slr', expanded_derivative, adapter_out) * rank_scale).astype(jnp.bfloat16))
        primary_derivative = jnp.einsum('igu,igl->iul', wide_sample_matrix, narrow_derivative.astype(jnp.float32)) * shrink_factor
        second_grad = jnp.einsum('slr,slk->srk', wide_low, expanded_derivative) * rank_scale
        per_seq = jnp.concatenate([primary_derivative.reshape(seq_dev, D * R), second_grad.reshape(seq_dev, R * KV)], axis=1)
        same_task = (block_tasks[:, None] == block_tasks[None, :]).astype(jnp.float32)
        merged_total = jnp.dot(same_task, per_seq, precision=lax.Precision.HIGHEST)
        repeated = lax.optimization_barrier(jnp.sum(same_task * earlier, axis=1)) > 0
        rounded = lax.optimization_barrier(merged_total.astype(jnp.bfloat16)).astype(jnp.float32)
        rounded = jnp.where(repeated[:, None], jnp.zeros_like(rounded), rounded)
        return (accumulated.at[block_tasks].add(rounded), None)
    adapter_grad, unused_out = lax.scan(one_block, jnp.zeros((TASKS, P_SIZE), jnp.float32), (token_blocks, teacher_blocks, blocks_per_task))
    return jnp.dot(task_codes.astype(jnp.float32).T, adapter_grad, precision=lax.Precision.HIGHEST)
```

```python
import math

import jax
import jax.numpy as jnp
from jax import lax
from jax.experimental import pallas as pl
from jax.experimental.pallas import tpu as pltpu
from jax.sharding import PartitionSpec as P

D = 5120
KV = 1024
R = 32
TPG = 4
SEQ_LEN = 128
GROUPS = 32
MEMBERS = 16
SIDE = 4
TASKS = 64
TOK = 256
BLK = D // MEMBERS
SLICE = BLK // SIDE
ROWS = 3 * TPG * GROUPS
PIECES = 2
PIECE = ROWS // PIECES
HALF = MEMBERS // 2
TALL = 192 * GROUPS
MESH = pl.DeviceIdType.MESH
F32 = jnp.float32
BF16 = jnp.bfloat16
LOSS_SCALE = 1.0 / math.sqrt(TOK * MEMBERS)
SHRINK = 1.0 / math.sqrt(D)
RANK_SCALE = 1.0 / math.sqrt(R)


def dot(a, b):
    return jnp.dot(a, b, preferred_element_type=F32)


def iota(shape, axis):
    return lax.broadcasted_iota(jnp.int32, shape, axis)


def step_kernel(
    codes_ref,
    hyper_ref,
    frozen_hbm,
    tokens_hbm,
    teacher_hbm,
    seq_ref,
    share_ref,
    counts_ref,
    out_ref,
    w_buf,
    tok_buf,
    teach_buf,
    perm_buf,
    stage,
    send_small,
    recv_small,
    send_back,
    recv_back,
    ag_buf,
    tall,
    low_rows,
    b_mat,
    acc,
    own,
    send_run,
    recv_run,
    local_sem,
    small_s,
    small_r,
    back_s,
    back_r,
    wz_s,
    wz_r,
    p1_s,
    p1_r,
    p2_s,
    p2_r,
    die_s,
    die_r,
    ag_s,
    ag_r,
    rs_s,
    rs_r,
):
    dp = lax.axis_index("dp")
    z = lax.axis_index("mp")
    c = lax.rem(dp, 2)
    x = lax.rem(dp // 2, SIDE)
    y = dp // (2 * SIDE)
    f = 1 - 2 * c

    def wrap(value, size):
        return lax.rem(value + 2 * size, size)

    def place(yy, xx):
        return (yy * SIDE + xx) * 2 + c

    def remote(src, dst, ssem, rsem, to_dp, to_z):
        return pltpu.make_async_remote_copy(
            src_ref=src,
            dst_ref=dst,
            send_sem=ssem,
            recv_sem=rsem,
            device_id=(to_dp, to_z),
            device_id_type=MESH,
        )

    sent = []

    def send(src, dst, ssem, rsem, to_dp, to_z):
        copy = remote(src, dst, ssem, rsem, to_dp, to_z)
        copy.start()
        sent.append(copy)

    def arrive(dst, ssem, rsem):
        remote(dst, dst, ssem, rsem, dp, z).wait_recv()

    barrier = pltpu.get_barrier_semaphore()

    @pl.loop(1, GROUPS)
    def _(i):
        pl.semaphore_signal(
            barrier, inc=1, device_id=(lax.rem(dp + i, GROUPS), z), device_id_type=MESH
        )

    for shift in (1, -1):
        pl.semaphore_signal(
            barrier, inc=1, device_id=(dp, wrap(z + shift, MEMBERS)), device_id_type=MESH
        )

    local = []
    for yy in range(SIDE):
        for cc in range(2):
            local.append(
                pltpu.make_async_copy(
                    frozen_hbm.at[:, pl.ds((2 * yy + cc) * 128, 128)],
                    w_buf.at[yy, cc, pl.ds(pl.multiple_of(BLK * z, 16), BLK), :],
                    local_sem.at[2 * yy + cc],
                )
            )
    tok_copy = pltpu.make_async_copy(tokens_hbm, tok_buf, local_sem.at[8])
    teach_copy = pltpu.make_async_copy(teacher_hbm, teach_buf, local_sem.at[9])
    for copy in local:
        copy.start()
    tok_copy.start()
    teach_copy.start()

    share = share_ref[...].astype(F32)
    g_row = lax.rem(iota((TPG * GROUPS, GROUPS), 0), GROUPS)
    g_col = iota((TPG * GROUPS, GROUPS), 1)
    share_all = jnp.broadcast_to(share, (TPG * GROUPS, GROUPS))
    first = jnp.sum(jnp.where(g_col < g_row, share_all, 0.0), axis=1, keepdims=True)
    mine = jnp.sum(jnp.where(g_col == g_row, share_all, 0.0), axis=1, keepdims=True)
    slot_row = (iota((TPG * GROUPS, TASKS), 0) // GROUPS).astype(F32)
    task_col = iota((TPG * GROUPS, TASKS), 1).astype(F32)
    picks = (task_col == first + slot_row) & (slot_row < mine)
    codes_sel = dot(jnp.where(picks, 1.0, 0.0).astype(BF16), codes_ref[...]).astype(BF16)
    stage[pl.ds(ROWS, 128), :] = jnp.zeros((128, 128), F32)
    for s in range(3):
        cols = dot(codes_sel, hyper_ref[:, 128 * s : 128 * (s + 1)]).astype(BF16).astype(F32)
        for slot in range(TPG):
            stage[pl.ds((slot * 3 + s) * GROUPS, GROUPS), :] = cols[
                slot * GROUPS : (slot + 1) * GROUPS
            ]

    @pl.loop(0, GROUPS)
    def _(g):
        send_small[g] = stage[pl.ds(g, 16, stride=GROUPS), :].astype(BF16)

    row = iota((512, 512), 0)
    target = lax.rem(row // 32, 4) * 128 + (row // 128) * 32 + lax.rem(row, 32)
    perm_buf[...] = jnp.where(iota((512, 512), 1) == target, 1.0, 0.0).astype(BF16)

    pl.semaphore_wait(barrier, GROUPS + 1)

    @pl.loop(1, GROUPS)
    def _(i):
        to = lax.rem(dp + i, GROUPS)
        remote(
            send_small.at[to], recv_small.at[dp], small_s.at[i], small_r.at[i], to, z
        ).start()

    for copy in local:
        copy.wait()

    def w_block(way, d):
        return wrap(z - f * d if way == 0 else z + f * d, MEMBERS)

    def w_rows(start, size):
        return pl.ds(pl.multiple_of(start, 16), size)

    def w_slice(zb):
        return w_buf.at[y, c, w_rows(BLK * zb + SLICE * x, SLICE), :]

    def w_piece(way, phase, zb, i):
        if way == 0 and phase == 1:
            return w_buf.at[y, c, w_rows(BLK * zb + SLICE * i, SLICE), :]
        if way == 0:
            return w_buf.at[i, c, w_rows(BLK * zb, BLK), :]
        if phase == 1:
            return w_buf.at[i, c, w_rows(BLK * zb + SLICE * x, SLICE), :]
        return w_buf.at[:, c, w_rows(BLK * zb + SLICE * i, SLICE), :]

    def along(way, phase):
        return x if (way == 0) == (phase == 1) else y

    def shifted(way, phase, by):
        if (way == 0) == (phase == 1):
            return place(y, wrap(x + by, SIDE))
        return place(wrap(y + by, SIDE), x)

    def w_reach(way):
        return HALF if way == 0 else HALF - 1

    def z_to(way):
        return wrap(z + f if way == 0 else z - f, MEMBERS)

    def send_z(way, d):
        ref = w_slice(w_block(way, d - 1))
        send(ref, ref, wz_s.at[way, d - 1], wz_r.at[way, d - 1], dp, z_to(way))

    def start_phase(way, phase, d):
        sems, semr = (p1_s, p1_r) if phase == 1 else (p2_s, p2_r)
        ref = w_piece(way, phase, w_block(way, d), along(way, phase))
        send(ref, ref, sems.at[way, d - 1, 0], semr.at[way, d - 1, 0], shifted(way, phase, f), z)
        send(ref, ref, sems.at[way, d - 1, 1], semr.at[way, d - 1, 1], shifted(way, phase, -f), z)

    def pass_on(way, phase, d):
        sems, semr = (p1_s, p1_r) if phase == 1 else (p2_s, p2_r)
        ref = w_piece(way, phase, w_block(way, d), wrap(along(way, phase) - f, SIDE))
        arrive(ref, sems.at[way, d - 1, 0], semr.at[way, d - 1, 0])
        send(ref, ref, sems.at[way, d - 1, 2], semr.at[way, d - 1, 2], shifted(way, phase, f), z)

    def end_phase(way, phase, d):
        sems, semr = (p1_s, p1_r) if phase == 1 else (p2_s, p2_r)
        zb = w_block(way, d)
        at = along(way, phase)
        arrive(
            w_piece(way, phase, zb, wrap(at + f, SIDE)),
            sems.at[way, d - 1, 1],
            semr.at[way, d - 1, 1],
        )
        arrive(
            w_piece(way, phase, zb, wrap(at - 2 * f, SIDE)),
            sems.at[way, d - 1, 2],
            semr.at[way, d - 1, 2],
        )

    def die_part(way, d, core):
        return w_buf.at[:, core, w_rows(BLK * w_block(way, d), BLK), :]

    def start_die(way, d):
        ref = die_part(way, d, c)
        send(ref, ref, die_s.at[way, d - 1], die_r.at[way, d - 1], dp + f, z)

    def end_die(way, d):
        other = wrap(z + f * d if way == 0 else z - f * d, MEMBERS)
        ref = w_buf.at[:, 1 - c, w_rows(BLK * other, BLK), :]
        arrive(ref, die_s.at[way, d - 1], die_r.at[way, d - 1])

    def ag_piece(way, d, p):
        return ag_buf.at[w_block(way, d), pl.ds(p * PIECE, PIECE), :]

    def send_ag(way, d, p):
        ref = ag_piece(way, d - 1, p)
        send(ref, ref, ag_s.at[way, d - 1, p], ag_r.at[way, d - 1, p], dp, z_to(way))

    def get_ag(way, d):
        for p in range(PIECES):
            arrive(ag_piece(way, d, p), ag_s.at[way, d - 1, p], ag_r.at[way, d - 1, p])
            if d < w_reach(way):
                send_ag(way, d + 1, p)

    def spread(m):
        block = jnp.concatenate(
            [ag_buf[m, pl.ds(96 * slot, 96), :] for slot in range(TPG)], axis=1
        )
        moved = dot(block, perm_buf[...])
        for s in range(3):
            for j in range(4):
                tall[pl.ds(12 * m + 4 * s + j, GROUPS, stride=192), :] = moved[
                    32 * s : 32 * (s + 1), 128 * j : 128 * (j + 1)
                ]
        for slot in range(TPG):
            for s in range(3):
                last = ag_buf[m, pl.ds(96 * slot + 32 * s + 16, 16), :].astype(F32)
                low_rows[slot, pl.ds(3 * m + s, 8, stride=48), :] = last[8:16]

    for way in (0, 1):
        send_z(way, 1)

    recv_small[dp] = send_small[dp]

    @pl.loop(1, GROUPS)
    def _(i):
        frm = wrap(dp - i, GROUPS)
        arrive(recv_small.at[frm], small_s.at[i], small_r.at[i])

    stage[...] = recv_small[...].astype(F32).reshape(GROUPS * 16, 128)
    for k in range(3 * TPG):
        ag_buf[z, pl.ds(32 * k, 32), :] = stage[pl.ds(k, GROUPS, stride=16), :].astype(BF16)

    for way in (0, 1):
        for p in range(PIECES):
            send_ag(way, 1, p)
    spread(z)

    ways = [(way, d) for d in range(1, HALF + 1) for way in (0, 1) if d <= w_reach(way)]

    def at(d):
        return [w for w in ways if w[1] == d]

    for t in range(1, HALF + 5):
        for way, d in at(t):
            ref = w_slice(w_block(way, d))
            arrive(ref, wz_s.at[way, d - 1], wz_r.at[way, d - 1])
            if d < w_reach(way):
                send_z(way, d + 1)
            start_phase(way, 1, d)
        for way, d in at(t - 1):
            pass_on(way, 1, d)
        for way, d in at(t):
            get_ag(way, d)
        for way, d in at(t - 1):
            end_phase(way, 1, d)
            start_phase(way, 2, d)
        for way, d in at(t):
            spread(w_block(way, d))
        for way, d in at(t - 2):
            pass_on(way, 2, d)
        for way, d in at(t - 3):
            end_phase(way, 2, d)
            start_die(way, d)

    tok_copy.wait()
    teach_copy.wait()
    seq0 = seq_ref[0]
    seq1 = seq_ref[1]
    upper = iota((TOK, 128), 0) < SEQ_LEN
    slot_of = jnp.where(upper, seq0, seq1)
    chosen = slot_of == iota((TOK, 128), 1) // R
    low_all = jnp.zeros((TOK, 128), F32)
    for k in range(8):
        low_all = low_all + dot(
            tok_buf[:, 640 * k : 640 * (k + 1)], tall[pl.ds(640 * k, 640), :].astype(BF16)
        )
    low = jnp.where(chosen, low_all * SHRINK, 0.0).astype(BF16)
    for slot in range(TPG):
        for k in range(8):
            b_mat[pl.ds(32 * slot, 32), 128 * k : 128 * (k + 1)] = low_rows[
                slot, pl.ds(128 + k, 32, stride=8), :
            ].astype(BF16)

    lane = iota((1, GROUPS), 1)
    own_first = jnp.sum(jnp.where(lane < dp, share, 0.0), axis=1, keepdims=True)
    counts = counts_ref[...].astype(F32)
    weights = (jnp.sum(counts, axis=1, keepdims=True) / TASKS) / counts
    task_lane = iota((1, TASKS), 1).astype(F32)

    def weight_of(slot):
        hit = task_lane == own_first + slot.astype(F32)
        return jnp.sum(jnp.where(hit, weights, 0.0), axis=1, keepdims=True) * LOSS_SCALE

    weight0 = weight_of(seq0)
    weight1 = weight_of(seq1)

    for q in range(SIDE):
        cols = pl.ds(256 * q, 256)
        acc[:, cols] = dot(low, b_mat[:, cols]) * RANK_SCALE - teach_buf[:, cols].astype(F32)

    for way, d in ways:
        end_die(way, d)

    for q in range(SIDE):
        cols = pl.ds(256 * q, 256)

        def body(k, total):
            rows = pl.ds(pl.multiple_of(640 * k, 128), 640)
            wide = jnp.concatenate([w_buf[q, 0, rows, :], w_buf[q, 1, rows, :]], axis=1)
            return total + dot(tok_buf[:, rows], wide)

        total = lax.fori_loop(0, 8, body, acc[:, cols])
        acc[:SEQ_LEN, cols] = total[:SEQ_LEN] * weight0
        acc[SEQ_LEN:, cols] = total[SEQ_LEN:] * weight1

    grad = acc[...].astype(BF16)
    low_grad = lax.dot_general(
        grad, b_mat[...], (((1,), (1,)), ((), ())), preferred_element_type=F32
    )
    low_grad = jnp.where(chosen, low_grad * RANK_SCALE, 0.0).astype(BF16)
    for k in range(8):
        tall[pl.ds(640 * k, 640), :] = (
            lax.dot_general(
                tok_buf[:, 640 * k : 640 * (k + 1)],
                low_grad,
                (((0,), (0,)), ((), ())),
                preferred_element_type=F32,
            )
            * SHRINK
        )
    tall[pl.ds(D, TALL - D), :] = jnp.zeros((TALL - D, 128), F32)
    second = (
        lax.dot_general(low, grad, (((0,), (0,)), ((), ())), preferred_element_type=F32)
        * RANK_SCALE
    )
    for slot in range(TPG):
        low_rows[slot, pl.ds(0, 128), :] = jnp.zeros((128, 128), F32)
        for k in range(8):
            low_rows[slot, pl.ds(128 + k, 32, stride=8), :] = second[
                32 * slot : 32 * (slot + 1), 128 * k : 128 * (k + 1)
            ]

    def collect(m):
        parts = [
            jnp.concatenate(
                [
                    tall[pl.ds(12 * m + 4 * s + j, GROUPS, stride=192), :].astype(BF16)
                    for j in range(4)
                ],
                axis=1,
            )
            for s in range(3)
        ]
        moved = dot(jnp.concatenate(parts, axis=0), perm_buf[...])
        for slot in range(TPG):
            for s in range(3):
                from_a = moved[32 * s : 32 * (s + 1), 128 * slot : 128 * (slot + 1)]
                from_b = low_rows[slot, pl.ds(3 * m + s, 8, stride=48), :]
                flat = 48 * (iota((8, 128), 0) + 24) + 3 * m + s
                tail = jnp.where(flat >= D * R // 128, from_b, from_a[24:])
                own[m, pl.ds(96 * slot + 32 * s, 32), :] = jnp.concatenate(
                    [from_a[:24], tail], axis=0
                ).astype(BF16)

    def rs_dest(way, k):
        return wrap(z + f * (HALF - k) if way == 0 else z - f * (HALF - 1 - k), MEMBERS)

    for k in range(HALF):
        for way in (0, 1):
            if k >= w_reach(way):
                continue
            m = rs_dest(way, k)
            collect(m)
            for p in range(PIECES):
                rows = pl.ds(p * PIECE, PIECE)
                if k == 0:
                    src = own.at[m, rows, :]
                else:
                    arrive(
                        recv_run.at[way, k - 1, rows, :],
                        rs_s.at[way, k - 1, p],
                        rs_r.at[way, k - 1, p],
                    )
                    send_run[way, k, rows, :] = (
                        recv_run[way, k - 1, rows, :].astype(F32) + own[m, rows, :].astype(F32)
                    ).astype(BF16)
                    src = send_run.at[way, k, rows, :]
                send(
                    src,
                    recv_run.at[way, k, rows, :],
                    rs_s.at[way, k, p],
                    rs_r.at[way, k, p],
                    dp,
                    z_to(way),
                )
    collect(z)
    for p in range(PIECES):
        rows = pl.ds(p * PIECE, PIECE)
        for way in (0, 1):
            k = w_reach(way) - 1
            arrive(recv_run.at[way, k, rows, :], rs_s.at[way, k, p], rs_r.at[way, k, p])
        stage[rows, :] = (
            recv_run[0, HALF - 1, rows, :].astype(F32)
            + recv_run[1, HALF - 2, rows, :].astype(F32)
            + own[z, rows, :].astype(F32)
        )
    stage[pl.ds(ROWS, 128), :] = jnp.zeros((128, 128), F32)

    @pl.loop(0, GROUPS)
    def _(g):
        send_back[g] = stage[pl.ds(g, 16, stride=GROUPS), :].astype(BF16)

    @pl.loop(1, GROUPS)
    def _(i):
        to = lax.rem(dp + i, GROUPS)
        remote(send_back.at[to], recv_back.at[dp], back_s.at[i], back_r.at[i], to, z).start()

    recv_back[dp] = send_back[dp]

    @pl.loop(1, GROUPS)
    def _(i):
        frm = wrap(dp - i, GROUPS)
        arrive(recv_back.at[frm], back_s.at[i], back_r.at[i])

    stage[...] = recv_back[...].astype(F32).reshape(GROUPS * 16, 128)
    for s in range(3):
        sums = jnp.concatenate(
            [stage[pl.ds(slot * 3 + s, GROUPS, stride=16), :] for slot in range(TPG)], axis=0
        ).astype(BF16)
        out_ref[:, 128 * s : 128 * (s + 1)] = lax.dot_general(
            codes_sel, sums, (((0,), (0,)), ((), ())), preferred_element_type=F32
        )

    for copy in sent:
        copy.wait_send()

    @pl.loop(1, GROUPS)
    def _(i):
        to = lax.rem(dp + i, GROUPS)
        remote(
            send_small.at[to], recv_small.at[dp], small_s.at[i], small_r.at[i], to, z
        ).wait_send()
        remote(
            send_back.at[to], recv_back.at[dp], back_s.at[i], back_r.at[i], to, z
        ).wait_send()


def shards(
    task_codes, hyper_weight, frozen_weight, tokens, teacher, seq_slot, task_share, token_counts
):
    vmem = pl.BlockSpec(memory_space=pltpu.VMEM)
    smem = pl.BlockSpec(memory_space=pltpu.SMEM)
    hbm = pl.BlockSpec(memory_space=pl.ANY)
    dma = pltpu.SemaphoreType.DMA
    small = pltpu.VMEM((GROUPS, 16, 128), BF16)
    return pl.pallas_call(
        step_kernel,
        out_shape=jax.ShapeDtypeStruct((128, 384), F32),
        in_specs=[vmem, vmem, hbm, hbm, hbm, smem, vmem, vmem],
        out_specs=vmem,
        scratch_shapes=[
            pltpu.VMEM((SIDE, 2, D, 128), BF16),
            pltpu.VMEM((TOK, D), BF16),
            pltpu.VMEM((TOK, KV), BF16),
            pltpu.VMEM((512, 512), BF16),
            pltpu.VMEM((512, 128), F32),
            small,
            small,
            small,
            small,
            pltpu.VMEM((MEMBERS, ROWS, 128), BF16),
            pltpu.VMEM((TALL, 128), F32),
            pltpu.VMEM((TPG, ROWS, 128), F32),
            pltpu.VMEM((128, KV), BF16),
            pltpu.VMEM((TOK, KV), F32),
            pltpu.VMEM((MEMBERS, ROWS, 128), BF16),
            pltpu.VMEM((2, HALF, ROWS, 128), BF16),
            pltpu.VMEM((2, HALF, ROWS, 128), BF16),
            dma((10,)),
            dma((GROUPS,)),
            dma((GROUPS,)),
            dma((GROUPS,)),
            dma((GROUPS,)),
            dma((2, HALF)),
            dma((2, HALF)),
            dma((2, HALF, 3)),
            dma((2, HALF, 3)),
            dma((2, HALF, 3)),
            dma((2, HALF, 3)),
            dma((2, HALF)),
            dma((2, HALF)),
            dma((2, HALF, PIECES)),
            dma((2, HALF, PIECES)),
            dma((2, HALF, PIECES)),
            dma((2, HALF, PIECES)),
        ],
        compiler_params=pltpu.CompilerParams(collective_id=0, has_side_effects=True),
    )(
        task_codes,
        hyper_weight,
        frozen_weight,
        tokens,
        teacher,
        seq_slot,
        task_share.reshape(1, -1),
        token_counts.reshape(1, -1),
    )


def solution(mesh):
    placed = (
        P(),
        P(None, ("dp", "mp")),
        P("mp", None),
        P(("dp", "mp"), None),
        P(("dp", "mp"), None),
        P(("dp", "mp")),
        P(),
        P(),
    )
    return jax.shard_map(
        shards, mesh=mesh, in_specs=placed, out_specs=P(None, ("dp", "mp")), check_vma=False
    )
```

```python
import math

import jax
import jax.numpy as jnp
from jax import lax
from jax.experimental import pallas as pl
from jax.experimental.pallas import tpu as pltpu
from jax.sharding import PartitionSpec as P

D = 5120
KV = 1024
R = 32
TPG = 4
SEQ_LEN = 128
GROUPS = 32
MEMBERS = 16
SIDE = 4
TASKS = 64
TOK = 256
BLK = D // MEMBERS
SLICE = BLK // SIDE
ROWS = 3 * TPG * GROUPS
PIECES = 2
PIECE = ROWS // PIECES
RS_PIECES = 4
RS_PIECE = ROWS // RS_PIECES
HALF = MEMBERS // 2
TALL = 192 * GROUPS
MESH = pl.DeviceIdType.MESH
F32 = jnp.float32
BF16 = jnp.bfloat16
LOSS_SCALE = 1.0 / math.sqrt(TOK * MEMBERS)
SHRINK = 1.0 / math.sqrt(D)
RANK_SCALE = 1.0 / math.sqrt(R)


def dot(a, b):
    return jnp.dot(a, b, preferred_element_type=F32)


def iota(shape, axis):
    return lax.broadcasted_iota(jnp.int32, shape, axis)


def step_kernel(
    codes_ref,
    hyper_ref,
    frozen_hbm,
    tokens_hbm,
    teacher_hbm,
    seq_ref,
    share_ref,
    counts_ref,
    out_ref,
    w_buf,
    tok_buf,
    teach_buf,
    tok_blocks,
    tok_t,
    grad_buf,
    perm_buf,
    stage,
    send_small,
    recv_small,
    send_back,
    recv_back,
    ag_buf,
    tall,
    low_rows,
    b_mat,
    acc,
    own,
    send_run,
    recv_run,
    local_sem,
    small_s,
    small_r,
    back_s,
    back_r,
    wz_s,
    wz_r,
    p1_s,
    p1_r,
    p2_s,
    p2_r,
    die_s,
    die_r,
    ag_s,
    ag_r,
    rs_s,
    rs_r,
):
    dp = lax.axis_index("dp")
    z = lax.axis_index("mp")
    c = lax.rem(dp, 2)
    x = lax.rem(dp // 2, SIDE)
    y = dp // (2 * SIDE)
    f = 1 - 2 * c

    def wrap(value, size):
        return lax.rem(value + 2 * size, size)

    def place(yy, xx):
        return (yy * SIDE + xx) * 2 + c

    def remote(src, dst, ssem, rsem, to_dp, to_z):
        return pltpu.make_async_remote_copy(
            src_ref=src,
            dst_ref=dst,
            send_sem=ssem,
            recv_sem=rsem,
            device_id=(to_dp, to_z),
            device_id_type=MESH,
        )

    sent = []

    def send(src, dst, ssem, rsem, to_dp, to_z):
        copy = remote(src, dst, ssem, rsem, to_dp, to_z)
        copy.start()
        sent.append(copy)

    def arrive(dst, ssem, rsem):
        remote(dst, dst, ssem, rsem, dp, z).wait_recv()

    barrier = pltpu.get_barrier_semaphore()

    @pl.loop(1, GROUPS)
    def _(i):
        pl.semaphore_signal(
            barrier, inc=1, device_id=(lax.rem(dp + i, GROUPS), z), device_id_type=MESH
        )

    for shift in (1, -1):
        pl.semaphore_signal(
            barrier, inc=1, device_id=(dp, wrap(z + shift, MEMBERS)), device_id_type=MESH
        )

    local = []
    for yy in range(SIDE):
        for cc in range(2):
            local.append(
                pltpu.make_async_copy(
                    frozen_hbm.at[:, pl.ds((2 * yy + cc) * 128, 128)],
                    w_buf.at[yy, cc, pl.ds(pl.multiple_of(BLK * z, 16), BLK), :],
                    local_sem.at[2 * yy + cc],
                )
            )
    tok_copy = pltpu.make_async_copy(tokens_hbm, tok_buf, local_sem.at[8])
    teach_copy = pltpu.make_async_copy(teacher_hbm, teach_buf, local_sem.at[9])
    for copy in local:
        copy.start()
    tok_copy.start()
    teach_copy.start()

    share = share_ref[...].astype(F32)
    g_row = lax.rem(iota((TPG * GROUPS, GROUPS), 0), GROUPS)
    g_col = iota((TPG * GROUPS, GROUPS), 1)
    share_all = jnp.broadcast_to(share, (TPG * GROUPS, GROUPS))
    first = jnp.sum(jnp.where(g_col < g_row, share_all, 0.0), axis=1, keepdims=True)
    mine = jnp.sum(jnp.where(g_col == g_row, share_all, 0.0), axis=1, keepdims=True)
    slot_row = (iota((TPG * GROUPS, TASKS), 0) // GROUPS).astype(F32)
    task_col = iota((TPG * GROUPS, TASKS), 1).astype(F32)
    picks = (task_col == first + slot_row) & (slot_row < mine)
    codes_sel = dot(jnp.where(picks, 1.0, 0.0).astype(BF16), codes_ref[...]).astype(BF16)
    stage[pl.ds(ROWS, 128), :] = jnp.zeros((128, 128), F32)
    for s in range(3):
        cols = dot(codes_sel, hyper_ref[:, 128 * s : 128 * (s + 1)]).astype(BF16).astype(F32)
        for slot in range(TPG):
            stage[pl.ds((slot * 3 + s) * GROUPS, GROUPS), :] = cols[
                slot * GROUPS : (slot + 1) * GROUPS
            ]

    for g in range(GROUPS):
        send_small[g] = stage[pl.ds(g, 16, stride=GROUPS), :].astype(BF16)

    pl.semaphore_wait(barrier, GROUPS + 1)

    def w_block(way, d):
        return wrap(z - f * d if way == 0 else z + f * d, MEMBERS)

    def w_rows(start, size):
        return pl.ds(pl.multiple_of(start, 16), size)

    def w_slice(zb):
        return w_buf.at[y, c, w_rows(BLK * zb + SLICE * x, SLICE), :]

    def w_piece(way, phase, zb, i):
        if way == 0 and phase == 1:
            return w_buf.at[y, c, w_rows(BLK * zb + SLICE * i, SLICE), :]
        if way == 0:
            return w_buf.at[i, c, w_rows(BLK * zb, BLK), :]
        if phase == 1:
            return w_buf.at[i, c, w_rows(BLK * zb + SLICE * x, SLICE), :]
        return w_buf.at[:, c, w_rows(BLK * zb + SLICE * i, SLICE), :]

    def along(way, phase):
        return x if (way == 0) == (phase == 1) else y

    def shifted(way, phase, by):
        if (way == 0) == (phase == 1):
            return place(y, wrap(x + by, SIDE))
        return place(wrap(y + by, SIDE), x)

    def w_reach(way):
        return HALF if way == 0 else HALF - 1

    def z_to(way):
        return wrap(z + f if way == 0 else z - f, MEMBERS)

    def send_z(way, d):
        ref = w_slice(w_block(way, d - 1))
        send(ref, ref, wz_s.at[way, d - 1], wz_r.at[way, d - 1], dp, z_to(way))

    def sems_of(phase, way, d, kind):
        if phase == 1:
            return p1_s.at[way, d - 1, kind], p1_r.at[way, d - 1, kind]
        return p2_s.at[way, d - 1, kind], p2_r.at[way, d - 1, kind]

    def plane_send(way, phase, d, frm, kind, by):
        ref = w_piece(way, phase, w_block(way, d), wrap(along(way, phase) + frm, SIDE))
        send(ref, ref, *sems_of(phase, way, d, kind), shifted(way, phase, by), z)

    def plane_wait(way, phase, d, frm, kind):
        ref = w_piece(way, phase, w_block(way, d), wrap(along(way, phase) + frm, SIDE))
        arrive(ref, *sems_of(phase, way, d, kind))

    def twin_send(way, d, frm, kind):
        ref = w_piece(way, 2, w_block(way, d), wrap(along(way, 2) + frm, SIDE))
        send(ref, ref, die_s.at[way, d - 1, kind], die_r.at[way, d - 1, kind], dp + f, z)

    def twin_block(way, d):
        return wrap(z + f * d if way == 0 else z - f * d, MEMBERS)

    def twin_wait(way, d):
        zb = twin_block(way, d)
        at_twin = along(way, 2)
        for kind, frm in enumerate((0, -f, f, -2 * f)):
            i = wrap(at_twin + (frm if kind == 0 else -frm), SIDE)
            if way == 0:
                ref = w_buf.at[i, 1 - c, w_rows(BLK * zb, BLK), :]
            else:
                ref = w_buf.at[:, 1 - c, w_rows(BLK * zb + SLICE * i, SLICE), :]
            arrive(ref, die_s.at[way, d - 1, kind], die_r.at[way, d - 1, kind])

    def take_z(way, d):
        ref = w_slice(w_block(way, d))
        arrive(ref, wz_s.at[way, d - 1], wz_r.at[way, d - 1])
        if d < w_reach(way):
            send_z(way, d + 1)
        plane_send(way, 1, d, 0, 0, f)
        plane_send(way, 1, d, 0, 1, -f)
        plane_send(way, 1, d, 0, 2, 2 * f)

    def start_second(way, d):
        plane_wait(way, 1, d, -f, 0)
        plane_wait(way, 1, d, f, 1)
        plane_wait(way, 1, d, -2 * f, 2)
        plane_send(way, 2, d, 0, 0, f)
        plane_send(way, 2, d, 0, 1, -f)
        twin_send(way, d, 0, 0)

    def relay_second(way, d):
        plane_wait(way, 2, d, -f, 0)
        plane_send(way, 2, d, -f, 2, f)
        twin_send(way, d, -f, 1)

    def end_second(way, d):
        plane_wait(way, 2, d, f, 1)
        twin_send(way, d, f, 2)
        plane_wait(way, 2, d, -2 * f, 2)
        twin_send(way, d, -2 * f, 3)

    def ag_piece(way, d, p):
        return ag_buf.at[w_block(way, d), pl.ds(p * PIECE, PIECE), :]

    def send_ag(way, d, p):
        ref = ag_piece(way, d - 1, p)
        send(ref, ref, ag_s.at[way, d - 1, p], ag_r.at[way, d - 1, p], dp, z_to(way))

    def get_ag(way, d):
        for p in range(PIECES):
            arrive(ag_piece(way, d, p), ag_s.at[way, d - 1, p], ag_r.at[way, d - 1, p])
            if d < w_reach(way):
                send_ag(way, d + 1, p)

    def spread(m):
        block = jnp.concatenate(
            [ag_buf[m, pl.ds(96 * slot, 96), :] for slot in range(TPG)], axis=1
        )
        moved = dot(block, perm_buf[...])
        for s in range(3):
            for j in range(4):
                tall[pl.ds(12 * m + 4 * s + j, GROUPS, stride=192), :] = moved[
                    32 * s : 32 * (s + 1), 128 * j : 128 * (j + 1)
                ]
        for slot in range(TPG):
            for s in range(3):
                last = ag_buf[m, pl.ds(96 * slot + 32 * s + 16, 16), :].astype(F32)
                low_rows[slot, pl.ds(3 * m + s, 8, stride=48), :] = last[8:16]

    for copy in local:
        copy.wait()
    for way in (0, 1):
        send_z(way, 1)

    @pl.loop(1, GROUPS)
    def _(i):
        to = lax.rem(dp + i, GROUPS)
        remote(
            send_small.at[to], recv_small.at[dp], small_s.at[i], small_r.at[i], to, z
        ).start()

    row = iota((512, 512), 0)
    target = ((row >> 5) & 3) * 128 + (row >> 7) * 32 + (row & 31)
    perm_buf[...] = jnp.where(iota((512, 512), 1) == target, 1.0, 0.0).astype(BF16)

    ways = [(way, d) for d in range(1, HALF + 1) for way in (0, 1) if d <= w_reach(way)]

    def at(d):
        return [w for w in ways if w[1] == d]

    for way, d in at(1):
        take_z(way, d)

    recv_small[dp] = send_small[dp]

    @pl.loop(1, GROUPS)
    def _(i):
        frm = wrap(dp - i, GROUPS)
        arrive(recv_small.at[frm], small_s.at[i], small_r.at[i])

    stage[...] = recv_small[...].astype(F32).reshape(GROUPS * 16, 128)
    for k in range(3 * TPG):
        ag_buf[z, pl.ds(32 * k, 32), :] = stage[pl.ds(k, GROUPS, stride=16), :].astype(BF16)

    for way in (0, 1):
        for p in range(PIECES):
            send_ag(way, 1, p)
    spread(z)

    def frozen(blocks):
        @pl.loop(0, SIDE)
        def _(q):
            cols = pl.ds(pl.multiple_of(256 * q, 256), 256)
            total = None
            for zb in blocks:
                rows = w_rows(BLK * zb, BLK)
                wide = jnp.concatenate([w_buf[q, 0, rows, :], w_buf[q, 1, rows, :]], axis=1)
                part = dot(tok_blocks[zb], wide)
                total = part if total is None else total + part
            acc[:, cols] = acc[:, cols] + total

    def prepare(k):
        for zb in (2 * k, 2 * k + 1):
            tok_blocks[zb] = tok_buf[:, BLK * zb : BLK * (zb + 1)]
        tok_t[pl.ds(2 * BLK * k, 2 * BLK), :] = tok_buf[:, 2 * BLK * k : 2 * BLK * (k + 1)].T

    tok_copy.wait()
    teach_copy.wait()

    def steps(t):
        for way, d in at(t):
            take_z(way, d)
        for way, d in at(t - 1):
            start_second(way, d)
        for way, d in at(t - 2):
            relay_second(way, d)
        for way, d in at(t - 3):
            end_second(way, d)

    def finish(t):
        for way, d in at(t):
            twin_wait(way, d)
        frozen([w_block(way, d) for way, d in at(t)])

    for t in range(2, HALF + 1):
        steps(t)
        for way, d in at(t - 1):
            get_ag(way, d)
        if t <= 5:
            prepare(2 * (t - 2))
            prepare(2 * (t - 2) + 1)
        for way, d in at(t - 1):
            spread(w_block(way, d))
        if t == 5:
            acc[...] = -teach_buf[...].astype(F32)
            frozen([z])
        if t > 5:
            finish(t - 5)
    steps(HALF + 1)
    for way, d in at(HALF):
        get_ag(way, d)
        spread(w_block(way, d))
    finish(HALF - 4)

    seq0 = seq_ref[0]
    seq1 = seq_ref[1]
    upper = iota((TOK, 128), 0) < SEQ_LEN
    slot_of = jnp.where(upper, seq0, seq1)
    chosen = slot_of == iota((TOK, 128), 1) // R
    low_all = jnp.zeros((TOK, 128), F32)
    for k in range(8):
        low_all = low_all + dot(
            tok_buf[:, 640 * k : 640 * (k + 1)], tall[pl.ds(640 * k, 640), :].astype(BF16)
        )
    low = jnp.where(chosen, low_all * SHRINK, 0.0).astype(BF16)
    for slot in range(TPG):
        for k in range(8):
            b_mat[pl.ds(32 * slot, 32), 128 * k : 128 * (k + 1)] = low_rows[
                slot, pl.ds(128 + k, 32, stride=8), :
            ].astype(BF16)

    lane = iota((1, GROUPS), 1)
    own_first = jnp.sum(jnp.where(lane < dp, share, 0.0), axis=1, keepdims=True)
    counts = counts_ref[...].astype(F32)
    weights = (jnp.sum(counts, axis=1, keepdims=True) / TASKS) / counts
    task_lane = iota((1, TASKS), 1).astype(F32)

    def weight_of(slot):
        hit = task_lane == own_first + slot.astype(F32)
        return jnp.sum(jnp.where(hit, weights, 0.0), axis=1, keepdims=True) * LOSS_SCALE

    weight0 = weight_of(seq0)
    weight1 = weight_of(seq1)

    steps(HALF + 2)
    for q in range(SIDE):
        cols = pl.ds(256 * q, 256)
        acc[:, cols] = acc[:, cols] + dot(low, b_mat[:, cols]) * RANK_SCALE
    finish(HALF - 3)
    finish(HALF - 2)
    steps(HALF + 3)
    finish(HALF - 1)
    finish(HALF)
    for q in range(SIDE):
        cols = pl.ds(256 * q, 256)
        grad_buf[:SEQ_LEN, cols] = (acc[:SEQ_LEN, cols] * weight0).astype(BF16)
        grad_buf[SEQ_LEN:, cols] = (acc[SEQ_LEN:, cols] * weight1).astype(BF16)

    grad = grad_buf[...]
    low_grad = lax.dot_general(
        grad, b_mat[...], (((1,), (1,)), ((), ())), preferred_element_type=F32
    )
    low_grad = jnp.where(chosen, low_grad * RANK_SCALE, 0.0).astype(BF16)
    for k in range(8):
        tall[pl.ds(640 * k, 640), :] = dot(tok_t[pl.ds(640 * k, 640), :], low_grad) * SHRINK
    tall[pl.ds(D, TALL - D), :] = jnp.zeros((TALL - D, 128), F32)
    second = (
        lax.dot_general(low, grad, (((0,), (0,)), ((), ())), preferred_element_type=F32)
        * RANK_SCALE
    )
    for slot in range(TPG):
        low_rows[slot, pl.ds(0, 128), :] = jnp.zeros((128, 128), F32)
        for k in range(8):
            low_rows[slot, pl.ds(128 + k, 32, stride=8), :] = second[
                32 * slot : 32 * (slot + 1), 128 * k : 128 * (k + 1)
            ]

    def collect(m):
        parts = [
            jnp.concatenate(
                [
                    tall[pl.ds(12 * m + 4 * s + j, GROUPS, stride=192), :].astype(BF16)
                    for j in range(4)
                ],
                axis=1,
            )
            for s in range(3)
        ]
        moved = dot(jnp.concatenate(parts, axis=0), perm_buf[...])
        for slot in range(TPG):
            for s in range(3):
                from_a = moved[32 * s : 32 * (s + 1), 128 * slot : 128 * (slot + 1)]
                from_b = low_rows[slot, pl.ds(3 * m + s, 8, stride=48), :]
                flat = 48 * (iota((8, 128), 0) + 24) + 3 * m + s
                tail = jnp.where(flat >= D * R // 128, from_b, from_a[24:])
                own[m, pl.ds(96 * slot + 32 * s, 32), :] = jnp.concatenate(
                    [from_a[:24], tail], axis=0
                ).astype(BF16)

    def rs_dest(way, k):
        return wrap(z + f * (HALF - k) if way == 0 else z - f * (HALF - 1 - k), MEMBERS)

    def run_send(way, k, p, src):
        send(
            src,
            recv_run.at[way, k, pl.ds(p * RS_PIECE, RS_PIECE), :],
            rs_s.at[way, k, p],
            rs_r.at[way, k, p],
            dp,
            z_to(way),
        )

    for way in (0, 1):
        m = rs_dest(way, 0)
        collect(m)
        for p in range(RS_PIECES):
            run_send(way, 0, p, own.at[m, pl.ds(p * RS_PIECE, RS_PIECE), :])
    for k in range(1, HALF):
        live = [way for way in (0, 1) if k < w_reach(way)]
        for way in live:
            collect(rs_dest(way, k))
        for p in range(RS_PIECES):
            rows = pl.ds(p * RS_PIECE, RS_PIECE)
            for way in live:
                arrive(
                    recv_run.at[way, k - 1, rows, :],
                    rs_s.at[way, k - 1, p],
                    rs_r.at[way, k - 1, p],
                )
                send_run[way, k, rows, :] = (
                    recv_run[way, k - 1, rows, :].astype(F32)
                    + own[rs_dest(way, k), rows, :].astype(F32)
                ).astype(BF16)
                run_send(way, k, p, send_run.at[way, k, rows, :])
    collect(z)
    for p in range(RS_PIECES):
        rows = pl.ds(p * RS_PIECE, RS_PIECE)
        for way in (0, 1):
            k = w_reach(way) - 1
            arrive(recv_run.at[way, k, rows, :], rs_s.at[way, k, p], rs_r.at[way, k, p])
        stage[rows, :] = (
            recv_run[0, HALF - 1, rows, :].astype(F32)
            + recv_run[1, HALF - 2, rows, :].astype(F32)
            + own[z, rows, :].astype(F32)
        )
    stage[pl.ds(ROWS, 128), :] = jnp.zeros((128, 128), F32)

    for g in range(GROUPS):
        send_back[g] = stage[pl.ds(g, 16, stride=GROUPS), :].astype(BF16)

    @pl.loop(1, GROUPS)
    def _(i):
        to = lax.rem(dp + i, GROUPS)
        remote(send_back.at[to], recv_back.at[dp], back_s.at[i], back_r.at[i], to, z).start()

    recv_back[dp] = send_back[dp]

    @pl.loop(1, GROUPS)
    def _(i):
        frm = wrap(dp - i, GROUPS)
        arrive(recv_back.at[frm], back_s.at[i], back_r.at[i])

    stage[...] = recv_back[...].astype(F32).reshape(GROUPS * 16, 128)
    for s in range(3):
        sums = jnp.concatenate(
            [stage[pl.ds(slot * 3 + s, GROUPS, stride=16), :] for slot in range(TPG)], axis=0
        ).astype(BF16)
        out_ref[:, 128 * s : 128 * (s + 1)] = lax.dot_general(
            codes_sel, sums, (((0,), (0,)), ((), ())), preferred_element_type=F32
        )

    for copy in sent:
        copy.wait_send()

    @pl.loop(1, GROUPS)
    def _(i):
        to = lax.rem(dp + i, GROUPS)
        remote(
            send_small.at[to], recv_small.at[dp], small_s.at[i], small_r.at[i], to, z
        ).wait_send()
        remote(
            send_back.at[to], recv_back.at[dp], back_s.at[i], back_r.at[i], to, z
        ).wait_send()


def shards(
    task_codes, hyper_weight, frozen_weight, tokens, teacher, seq_slot, task_share, token_counts
):
    vmem = pl.BlockSpec(memory_space=pltpu.VMEM)
    smem = pl.BlockSpec(memory_space=pltpu.SMEM)
    hbm = pl.BlockSpec(memory_space=pl.ANY)
    dma = pltpu.SemaphoreType.DMA
    small = pltpu.VMEM((GROUPS, 16, 128), BF16)
    return pl.pallas_call(
        step_kernel,
        out_shape=jax.ShapeDtypeStruct((128, 384), F32),
        in_specs=[vmem, vmem, hbm, hbm, hbm, smem, vmem, vmem],
        out_specs=vmem,
        scratch_shapes=[
            pltpu.VMEM((SIDE, 2, D, 128), BF16),
            pltpu.VMEM((TOK, D), BF16),
            pltpu.VMEM((TOK, KV), BF16),
            pltpu.VMEM((MEMBERS, TOK, BLK), BF16),
            pltpu.VMEM((D, TOK), BF16),
            pltpu.VMEM((TOK, KV), BF16),
            pltpu.VMEM((512, 512), BF16),
            pltpu.VMEM((512, 128), F32),
            small,
            small,
            small,
            small,
            pltpu.VMEM((MEMBERS, ROWS, 128), BF16),
            pltpu.VMEM((TALL, 128), F32),
            pltpu.VMEM((TPG, ROWS, 128), F32),
            pltpu.VMEM((128, KV), BF16),
            pltpu.VMEM((TOK, KV), F32),
            pltpu.VMEM((MEMBERS, ROWS, 128), BF16),
            pltpu.VMEM((2, HALF, ROWS, 128), BF16),
            pltpu.VMEM((2, HALF, ROWS, 128), BF16),
            dma((10,)),
            dma((GROUPS,)),
            dma((GROUPS,)),
            dma((GROUPS,)),
            dma((GROUPS,)),
            dma((2, HALF)),
            dma((2, HALF)),
            dma((2, HALF, 3)),
            dma((2, HALF, 3)),
            dma((2, HALF, 3)),
            dma((2, HALF, 3)),
            dma((2, HALF, 4)),
            dma((2, HALF, 4)),
            dma((2, HALF, PIECES)),
            dma((2, HALF, PIECES)),
            dma((2, HALF, RS_PIECES)),
            dma((2, HALF, RS_PIECES)),
        ],
        compiler_params=pltpu.CompilerParams(collective_id=0, has_side_effects=True),
    )(
        task_codes,
        hyper_weight,
        frozen_weight,
        tokens,
        teacher,
        seq_slot,
        task_share.reshape(1, -1),
        token_counts.reshape(1, -1),
    )


def solution(mesh):
    placed = (
        P(),
        P(None, ("dp", "mp")),
        P("mp", None),
        P(("dp", "mp"), None),
        P(("dp", "mp"), None),
        P(("dp", "mp")),
        P(),
        P(),
    )
    return jax.shard_map(
        shards, mesh=mesh, in_specs=placed, out_specs=P(None, ("dp", "mp")), check_vma=False
    )
```

```python
import math

import jax
import jax.numpy as jnp
from jax import lax
from jax.experimental import pallas as pl
from jax.experimental.pallas import tpu as pltpu
from jax.sharding import PartitionSpec as P

D = 5120
KV = 1024
R = 32
TPG = 4
SEQ_LEN = 128
GROUPS = 32
MEMBERS = 16
SIDE = 4
TASKS = 64
TOK = 256
BLK = D // MEMBERS
SLICE = BLK // SIDE
ROWS = 3 * TPG * GROUPS
PIECES = 4
PIECE = ROWS // PIECES
RS_PIECES = 4
RS_PIECE = ROWS // RS_PIECES
HALF = MEMBERS // 2
TALL = 192 * GROUPS
MESH = pl.DeviceIdType.MESH
F32 = jnp.float32
BF16 = jnp.bfloat16
LOSS_SCALE = 1.0 / math.sqrt(TOK * MEMBERS)
SHRINK = 1.0 / math.sqrt(D)
RANK_SCALE = 1.0 / math.sqrt(R)


PLANE = sorted(
    (
        (dy, dx, dc)
        for dy in range(SIDE)
        for dx in range(SIDE)
        for dc in range(2)
        if dy or dx or dc
    ),
    key=lambda o: (-min(o[0], SIDE - o[0]) - min(o[1], SIDE - o[1]), o),
)


def dot(a, b):
    return jnp.dot(a, b, preferred_element_type=F32)


def iota(shape, axis):
    return lax.broadcasted_iota(jnp.int32, shape, axis)


def step_kernel(
    codes_hbm,
    hyper_hbm,
    frozen_hbm,
    tokens_hbm,
    teacher_hbm,
    seq_ref,
    share_ref,
    counts_ref,
    out_ref,
    codes_ref,
    hyper_ref,
    w_buf,
    tok_buf,
    teach_buf,
    tok_blocks,
    tok_t,
    grad_buf,
    perm_buf,
    stage,
    send_small,
    recv_small,
    send_back,
    recv_back,
    ag_buf,
    tall,
    low_rows,
    b_mat,
    acc,
    own,
    send_run,
    recv_run,
    local_sem,
    small_r,
    back_r,
    out_s,
    wz_r,
    p1_r,
    p2_r,
    die_r,
    ag_r,
    rs_r,
):
    dp = lax.axis_index("dp")
    z = lax.axis_index("mp")
    c = lax.rem(dp, 2)
    x = lax.rem(dp // 2, SIDE)
    y = dp // (2 * SIDE)
    f = 1 - 2 * c

    def wrap(value, size):
        return lax.rem(value + 2 * size, size)

    def place(yy, xx):
        return (yy * SIDE + xx) * 2 + c

    def remote(src, dst, ssem, rsem, to_dp, to_z):
        return pltpu.make_async_remote_copy(
            src_ref=src,
            dst_ref=dst,
            send_sem=ssem,
            recv_sem=rsem,
            device_id=(to_dp, to_z),
            device_id_type=MESH,
        )

    small_s, back_s, wz_s, p1_s, p2_s, die_s, ag_s, rs_s = (out_s.at[i] for i in range(8))

    def send(src, dst, ssem, rsem, to_dp, to_z):
        remote(src, dst, ssem, rsem, to_dp, to_z).start()

    def arrive(dst, rsem):
        remote(dst, dst, out_s.at[0], rsem, dp, z).wait_recv()

    def all_sent(like, ssem):
        remote(like, like, ssem, small_r, dp, z).wait_send()

    codes_copy = pltpu.make_async_copy(codes_hbm, codes_ref, local_sem.at[3])
    hyper_copy = pltpu.make_async_copy(hyper_hbm, hyper_ref, local_sem.at[4])
    codes_copy.start()
    hyper_copy.start()

    barrier = pltpu.get_barrier_semaphore()

    def peer(offset, sign):
        dy, dx, dc = offset
        core = c if dc == 0 else 1 - c
        return (wrap(y + sign * dy, SIDE) * SIDE + wrap(x + sign * dx, SIDE)) * 2 + core

    for offset in PLANE:
        pl.semaphore_signal(barrier, inc=1, device_id=(peer(offset, 1), z), device_id_type=MESH)

    for shift in (1, -1):
        pl.semaphore_signal(
            barrier, inc=1, device_id=(dp, wrap(z + shift, MEMBERS)), device_id_type=MESH
        )

    local = []
    for yy in range(SIDE):
        for cc in range(2):
            local.append(
                pltpu.make_async_copy(
                    frozen_hbm.at[:, pl.ds((2 * yy + cc) * 128, 128)],
                    w_buf.at[yy, cc, pl.ds(pl.multiple_of(BLK * z, 16), BLK), :],
                    local_sem.at[0],
                )
            )
    tok_copy = pltpu.make_async_copy(tokens_hbm, tok_buf, local_sem.at[1])
    teach_copy = pltpu.make_async_copy(teacher_hbm, teach_buf, local_sem.at[2])
    for copy in local:
        copy.start()
    tok_copy.start()
    teach_copy.start()

    share = share_ref[...].astype(F32)
    g_row = lax.rem(iota((TPG * GROUPS, GROUPS), 0), GROUPS)
    g_col = iota((TPG * GROUPS, GROUPS), 1)
    share_all = jnp.broadcast_to(share, (TPG * GROUPS, GROUPS))
    first = jnp.sum(jnp.where(g_col < g_row, share_all, 0.0), axis=1, keepdims=True)
    mine = jnp.sum(jnp.where(g_col == g_row, share_all, 0.0), axis=1, keepdims=True)
    slot_row = (iota((TPG * GROUPS, TASKS), 0) // GROUPS).astype(F32)
    task_col = iota((TPG * GROUPS, TASKS), 1).astype(F32)
    picks = (task_col == first + slot_row) & (slot_row < mine)
    codes_copy.wait()
    hyper_copy.wait()
    codes_sel = dot(jnp.where(picks, 1.0, 0.0).astype(BF16), codes_ref[...]).astype(BF16)
    stage[pl.ds(ROWS, 128), :] = jnp.zeros((128, 128), F32)
    for s in range(3):
        cols = dot(codes_sel, hyper_ref[:, 128 * s : 128 * (s + 1)]).astype(BF16).astype(F32)
        for slot in range(TPG):
            stage[pl.ds((slot * 3 + s) * GROUPS, GROUPS), :] = cols[
                slot * GROUPS : (slot + 1) * GROUPS
            ]

    for g in range(GROUPS):
        send_small[g] = stage[pl.ds(g, 16, stride=GROUPS), :].astype(BF16)

    pl.semaphore_wait(barrier, GROUPS + 1)

    def w_block(way, d):
        return wrap(z - f * d if way == 0 else z + f * d, MEMBERS)

    def w_rows(start, size):
        return pl.ds(pl.multiple_of(start, 16), size)

    def w_slice(zb):
        return w_buf.at[y, c, w_rows(BLK * zb + SLICE * x, SLICE), :]

    def w_piece(way, phase, zb, i):
        if way == 0 and phase == 1:
            return w_buf.at[y, c, w_rows(BLK * zb + SLICE * i, SLICE), :]
        if way == 0:
            return w_buf.at[i, c, w_rows(BLK * zb, BLK), :]
        if phase == 1:
            return w_buf.at[i, c, w_rows(BLK * zb + SLICE * x, SLICE), :]
        return w_buf.at[:, c, w_rows(BLK * zb + SLICE * i, SLICE), :]

    def along(way, phase):
        return x if (way == 0) == (phase == 1) else y

    def shifted(way, phase, by):
        if (way == 0) == (phase == 1):
            return place(y, wrap(x + by, SIDE))
        return place(wrap(y + by, SIDE), x)

    def w_reach(way):
        return HALF if way == 0 else HALF - 1

    def z_to(way):
        return wrap(z + f if way == 0 else z - f, MEMBERS)

    def send_z(way, d):
        ref = w_slice(w_block(way, d - 1))
        send(ref, ref, wz_s, wz_r.at[way, d - 1], dp, z_to(way))

    def plane_send(way, phase, d, frm, kind, by):
        ref = w_piece(way, phase, w_block(way, d), wrap(along(way, phase) + frm, SIDE))
        if phase == 1:
            ssem, rsem = p1_s, p1_r.at[way, d - 1]
        else:
            ssem, rsem = p2_s, p2_r.at[way, d - 1, min(kind, 1)]
        send(ref, ref, ssem, rsem, shifted(way, phase, by), z)

    def twin_send(way, d, frm):
        ref = w_piece(way, 2, w_block(way, d), wrap(along(way, 2) + frm, SIDE))
        send(ref, ref, die_s, die_r.at[way, d - 1], dp + f, z)

    def twin_block(way, d):
        return wrap(z + f * d if way == 0 else z - f * d, MEMBERS)

    def twin_wait(way, d):
        arrive(
            w_buf.at[:, 1 - c, w_rows(BLK * twin_block(way, d), BLK), :], die_r.at[way, d - 1]
        )

    def take_z(way, d):
        ref = w_slice(w_block(way, d))
        arrive(ref, wz_r.at[way, d - 1])
        if d < w_reach(way):
            send_z(way, d + 1)
        plane_send(way, 1, d, 0, 0, f)
        plane_send(way, 1, d, 0, 1, -f)
        plane_send(way, 1, d, 0, 2, 2 * f)

    def start_second(way, d):
        arrive(w_buf.at[0, c, pl.ds(0, 3 * SLICE), :], p1_r.at[way, d - 1])
        plane_send(way, 2, d, 0, 0, f)
        plane_send(way, 2, d, 0, 1, -f)
        twin_send(way, d, 0)

    def relay_second(way, d):
        arrive(
            w_piece(way, 2, w_block(way, d), wrap(along(way, 2) - f, SIDE)), p2_r.at[way, d - 1, 0]
        )
        plane_send(way, 2, d, -f, 2, f)
        twin_send(way, d, -f)

    def end_second(way, d):
        arrive(w_buf.at[0, c, pl.ds(0, 2 * BLK), :], p2_r.at[way, d - 1, 1])
        twin_send(way, d, f)
        twin_send(way, d, -2 * f)

    def ag_piece(way, d, p):
        return ag_buf.at[w_block(way, d), pl.ds(p * PIECE, PIECE), :]

    def send_ag(way, d, p):
        ref = ag_piece(way, d - 1, p)
        send(ref, ref, ag_s, ag_r.at[way, d - 1, p], dp, z_to(way))

    def get_ag(way, d, p):
        arrive(ag_piece(way, d, p), ag_r.at[way, d - 1, p])
        if d < w_reach(way):
            send_ag(way, d + 1, p)

    def spread(m):
        block = jnp.concatenate(
            [ag_buf[m, pl.ds(96 * slot, 96), :] for slot in range(TPG)], axis=1
        )
        moved = dot(block, perm_buf[...])
        for s in range(3):
            for j in range(4):
                tall[pl.ds(12 * m + 4 * s + j, GROUPS, stride=192), :] = moved[
                    32 * s : 32 * (s + 1), 128 * j : 128 * (j + 1)
                ]
        for slot in range(TPG):
            for s in range(3):
                last = ag_buf[m, pl.ds(96 * slot + 32 * s + 16, 16), :].astype(F32)
                low_rows[slot, pl.ds(3 * m + s, 8, stride=48), :] = last[8:16]

    own_rows = w_buf.at[:, :, w_rows(BLK * z, BLK), :]
    pltpu.make_async_copy(own_rows, own_rows, local_sem.at[0]).wait()
    for way in (0, 1):
        send_z(way, 1)

    def exchange(out, into, ssem, rsem):
        for offset in PLANE:
            to = peer(offset, 1)
            send(out.at[to], into.at[dp], ssem, rsem, to, z)

    def exchanged(into, rsem):
        arrive(into.at[pl.ds(0, GROUPS - 1)], rsem)

    exchange(send_small, recv_small, small_s, small_r)

    row = iota((512, 512), 0)
    target = ((row >> 5) & 3) * 128 + (row >> 7) * 32 + (row & 31)
    perm_buf[...] = jnp.where(iota((512, 512), 1) == target, 1.0, 0.0).astype(BF16)

    ways = [(way, d) for d in range(1, HALF + 1) for way in (0, 1) if d <= w_reach(way)]

    def at(d):
        return [w for w in ways if w[1] == d]

    def frozen(blocks):
        @pl.loop(0, SIDE)
        def _(q):
            cols = pl.ds(pl.multiple_of(256 * q, 256), 256)
            total = None
            for zb in blocks:
                rows = w_rows(BLK * zb, BLK)
                wide = jnp.concatenate([w_buf[q, 0, rows, :], w_buf[q, 1, rows, :]], axis=1)
                part = dot(tok_blocks[zb], wide)
                total = part if total is None else total + part
            acc[:, cols] = acc[:, cols] + total

    def prepare(k):
        for zb in (2 * k, 2 * k + 1):
            tok_blocks[zb] = tok_buf[:, BLK * zb : BLK * (zb + 1)]
        tok_t[pl.ds(2 * BLK * k, 2 * BLK), :] = tok_buf[:, 2 * BLK * k : 2 * BLK * (k + 1)].T

    tok_copy.wait()
    teach_copy.wait()
    for k in range(MEMBERS // 2):
        prepare(k)
    acc[...] = -teach_buf[...].astype(F32)

    for way, d in at(1):
        take_z(way, d)

    recv_small[dp] = send_small[dp]

    exchanged(recv_small, small_r)

    stage[...] = recv_small[...].astype(F32).reshape(GROUPS * 16, 128)
    for k in range(3 * TPG):
        ag_buf[z, pl.ds(32 * k, 32), :] = stage[pl.ds(k, GROUPS, stride=16), :].astype(BF16)

    for way in (0, 1):
        for p in range(PIECES):
            send_ag(way, 1, p)
    spread(z)

    frozen([z])

    def get_piece(t, p):
        for way, d in at(t - 1):
            get_ag(way, d, p)

    def steps(t):
        get_piece(t, 0)
        for way, d in at(t):
            take_z(way, d)
        for way, d in at(t - 1):
            start_second(way, d)
        get_piece(t, 1)
        for way, d in at(t - 3):
            relay_second(way, d)
        get_piece(t, 2)
        for way, d in at(t - 5):
            end_second(way, d)
        for way, d in at(t - 2):
            spread(w_block(way, d))
        get_piece(t, 3)

    def finish(*distances):
        blocks = [wd for d in distances for wd in at(d)]
        for way, d in blocks:
            twin_wait(way, d)
        frozen([w_block(way, d) for way, d in blocks])

    for t in range(2, HALF + 3):
        steps(t)
        if t == 8:
            finish(1, 2)
        if t == 10:
            finish(3, 4)

    steps(HALF + 3)

    seq0 = seq_ref[0]
    seq1 = seq_ref[1]
    upper = iota((TOK, 128), 0) < SEQ_LEN
    slot_of = jnp.where(upper, seq0, seq1)
    chosen = slot_of == iota((TOK, 128), 1) // R
    low_all = jnp.zeros((TOK, 128), F32)
    for k in range(8):
        low_all = low_all + dot(
            tok_buf[:, 640 * k : 640 * (k + 1)], tall[pl.ds(640 * k, 640), :].astype(BF16)
        )
    low = jnp.where(chosen, low_all * SHRINK, 0.0).astype(BF16)
    for slot in range(TPG):
        for k in range(8):
            b_mat[pl.ds(32 * slot, 32), 128 * k : 128 * (k + 1)] = low_rows[
                slot, pl.ds(128 + k, 32, stride=8), :
            ].astype(BF16)

    lane = iota((1, GROUPS), 1)
    own_first = jnp.sum(jnp.where(lane < dp, share, 0.0), axis=1, keepdims=True)
    counts = counts_ref[...].astype(F32)
    weights = (jnp.sum(counts, axis=1, keepdims=True) / TASKS) / counts
    task_lane = iota((1, TASKS), 1).astype(F32)

    def weight_of(slot):
        hit = task_lane == own_first + slot.astype(F32)
        return jnp.sum(jnp.where(hit, weights, 0.0), axis=1, keepdims=True) * LOSS_SCALE

    weight0 = weight_of(seq0)
    weight1 = weight_of(seq1)

    for q in range(SIDE):
        cols = pl.ds(256 * q, 256)
        acc[:, cols] = acc[:, cols] + dot(low, b_mat[:, cols]) * RANK_SCALE
    steps(HALF + 4)
    finish(5, 6)
    finish(7)
    steps(HALF + 5)
    finish(8)
    for q in range(SIDE):
        cols = pl.ds(256 * q, 256)
        grad_buf[:SEQ_LEN, cols] = (acc[:SEQ_LEN, cols] * weight0).astype(BF16)
        grad_buf[SEQ_LEN:, cols] = (acc[SEQ_LEN:, cols] * weight1).astype(BF16)

    grad = grad_buf[...]
    low_grad = lax.dot_general(
        grad, b_mat[...], (((1,), (1,)), ((), ())), preferred_element_type=F32
    )
    low_grad = jnp.where(chosen, low_grad * RANK_SCALE, 0.0).astype(BF16)
    for k in range(8):
        tall[pl.ds(640 * k, 640), :] = dot(tok_t[pl.ds(640 * k, 640), :], low_grad) * SHRINK
    tall[pl.ds(D, TALL - D), :] = jnp.zeros((TALL - D, 128), F32)
    second = (
        lax.dot_general(low, grad, (((0,), (0,)), ((), ())), preferred_element_type=F32)
        * RANK_SCALE
    )
    for slot in range(TPG):
        low_rows[slot, pl.ds(0, 128), :] = jnp.zeros((128, 128), F32)
        for k in range(8):
            low_rows[slot, pl.ds(128 + k, 32, stride=8), :] = second[
                32 * slot : 32 * (slot + 1), 128 * k : 128 * (k + 1)
            ]

    def collect(m):
        parts = [
            jnp.concatenate(
                [
                    tall[pl.ds(12 * m + 4 * s + j, GROUPS, stride=192), :].astype(BF16)
                    for j in range(4)
                ],
                axis=1,
            )
            for s in range(3)
        ]
        moved = dot(jnp.concatenate(parts, axis=0), perm_buf[...])
        for slot in range(TPG):
            for s in range(3):
                from_a = moved[32 * s : 32 * (s + 1), 128 * slot : 128 * (slot + 1)]
                from_b = low_rows[slot, pl.ds(3 * m + s, 8, stride=48), :]
                flat = 48 * (iota((8, 128), 0) + 24) + 3 * m + s
                tail = jnp.where(flat >= D * R // 128, from_b, from_a[24:])
                own[m, pl.ds(96 * slot + 32 * s, 32), :] = jnp.concatenate(
                    [from_a[:24], tail], axis=0
                ).astype(BF16)

    def rs_dest(way, k):
        return wrap(z + f * (HALF - k) if way == 0 else z - f * (HALF - 1 - k), MEMBERS)

    def run_send(way, k, p, src):
        send(
            src,
            recv_run.at[way, k, pl.ds(p * RS_PIECE, RS_PIECE), :],
            rs_s,
            rs_r.at[way, k, p],
            dp,
            z_to(way),
        )

    for way in (0, 1):
        m = rs_dest(way, 0)
        collect(m)
        for p in range(RS_PIECES):
            run_send(way, 0, p, own.at[m, pl.ds(p * RS_PIECE, RS_PIECE), :])
    for k in range(1, HALF):
        live = [way for way in (0, 1) if k < w_reach(way)]
        for way in live:
            collect(rs_dest(way, k))
        for p in range(RS_PIECES):
            rows = pl.ds(p * RS_PIECE, RS_PIECE)
            for way in live:
                arrive(recv_run.at[way, k - 1, rows, :], rs_r.at[way, k - 1, p])
                send_run[way, k, rows, :] = (
                    recv_run[way, k - 1, rows, :].astype(F32)
                    + own[rs_dest(way, k), rows, :].astype(F32)
                ).astype(BF16)
                run_send(way, k, p, send_run.at[way, k, rows, :])
    collect(z)
    for p in range(RS_PIECES):
        rows = pl.ds(p * RS_PIECE, RS_PIECE)
        for way in (0, 1):
            k = w_reach(way) - 1
            arrive(recv_run.at[way, k, rows, :], rs_r.at[way, k, p])
        stage[rows, :] = (
            recv_run[0, HALF - 1, rows, :].astype(F32)
            + recv_run[1, HALF - 2, rows, :].astype(F32)
            + own[z, rows, :].astype(F32)
        )
    stage[pl.ds(ROWS, 128), :] = jnp.zeros((128, 128), F32)

    for g in range(GROUPS):
        send_back[g] = stage[pl.ds(g, 16, stride=GROUPS), :].astype(BF16)

    exchange(send_back, recv_back, back_s, back_r)
    all_sent(send_small.at[pl.ds(0, GROUPS - 1)], small_s)
    all_sent(w_buf.at[0, 0, pl.ds(0, 15 * SLICE), :], wz_s)
    all_sent(w_buf.at[0, 0, pl.ds(0, 45 * SLICE), :], p1_s)
    all_sent(w_buf.at[:, 0, pl.ds(0, 45 * SLICE), :], p2_s)
    all_sent(w_buf.at[:, 0, pl.ds(0, 60 * SLICE), :], die_s)
    all_sent(ag_buf.at[pl.ds(0, 15)], ag_s)
    all_sent(own.at[pl.ds(0, 15)], rs_s)

    recv_back[dp] = send_back[dp]
    exchanged(recv_back, back_r)

    stage[...] = recv_back[...].astype(F32).reshape(GROUPS * 16, 128)
    for s in range(3):
        sums = jnp.concatenate(
            [stage[pl.ds(slot * 3 + s, GROUPS, stride=16), :] for slot in range(TPG)], axis=0
        ).astype(BF16)
        out_ref[:, 128 * s : 128 * (s + 1)] = lax.dot_general(
            codes_sel, sums, (((0,), (0,)), ((), ())), preferred_element_type=F32
        )

    all_sent(send_back.at[pl.ds(0, GROUPS - 1)], back_s)


def shards(
    task_codes, hyper_weight, frozen_weight, tokens, teacher, seq_slot, task_share, token_counts
):
    vmem = pl.BlockSpec(memory_space=pltpu.VMEM)
    smem = pl.BlockSpec(memory_space=pltpu.SMEM)
    hbm = pl.BlockSpec(memory_space=pl.ANY)
    dma = pltpu.SemaphoreType.DMA
    small = pltpu.VMEM((GROUPS, 16, 128), BF16)
    return pl.pallas_call(
        step_kernel,
        out_shape=jax.ShapeDtypeStruct((128, 384), F32),
        in_specs=[hbm, hbm, hbm, hbm, hbm, smem, vmem, vmem],
        out_specs=vmem,
        scratch_shapes=[
            pltpu.VMEM((TASKS, 128), BF16),
            pltpu.VMEM((128, 384), BF16),
            pltpu.VMEM((SIDE, 2, D, 128), BF16),
            pltpu.VMEM((TOK, D), BF16),
            pltpu.VMEM((TOK, KV), BF16),
            pltpu.VMEM((MEMBERS, TOK, BLK), BF16),
            pltpu.VMEM((D, TOK), BF16),
            pltpu.VMEM((TOK, KV), BF16),
            pltpu.VMEM((512, 512), BF16),
            pltpu.VMEM((512, 128), F32),
            small,
            small,
            small,
            small,
            pltpu.VMEM((MEMBERS, ROWS, 128), BF16),
            pltpu.VMEM((TALL, 128), F32),
            pltpu.VMEM((TPG, ROWS, 128), F32),
            pltpu.VMEM((128, KV), BF16),
            pltpu.VMEM((TOK, KV), F32),
            pltpu.VMEM((MEMBERS, ROWS, 128), BF16),
            pltpu.VMEM((2, HALF, ROWS, 128), BF16),
            pltpu.VMEM((2, HALF, ROWS, 128), BF16),
            dma((5,)),
            dma,
            dma,
            dma((8,)),
            dma((2, HALF)),
            dma((2, HALF)),
            dma((2, HALF, 2)),
            dma((2, HALF)),
            dma((2, HALF, PIECES)),
            dma((2, HALF, RS_PIECES)),
        ],
        compiler_params=pltpu.CompilerParams(collective_id=0, has_side_effects=True),
    )(
        task_codes,
        hyper_weight,
        frozen_weight,
        tokens,
        teacher,
        seq_slot,
        task_share.reshape(1, -1),
        token_counts.reshape(1, -1),
    )


def solution(mesh):
    placed = (
        P(),
        P(None, ("dp", "mp")),
        P("mp", None),
        P(("dp", "mp"), None),
        P(("dp", "mp"), None),
        P(("dp", "mp")),
        P(),
        P(),
    )
    return jax.shard_map(
        shards, mesh=mesh, in_specs=placed, out_specs=P(None, ("dp", "mp")), check_vma=False
    )
```

```python
import math

import jax
import jax.numpy as jnp
from jax import lax
from jax.experimental import pallas as pl
from jax.experimental.pallas import tpu as pltpu
from jax.sharding import PartitionSpec as P

D = 5120
KV = 1024
R = 32
TPG = 4
SEQ_LEN = 128
GROUPS = 32
MEMBERS = 16
SIDE = 4
TASKS = 64
TOK = 256
BLK = D // MEMBERS
SLICE = BLK // SIDE
ROWS = 3 * TPG * GROUPS
PIECES = 4
PIECE = ROWS // PIECES
RS_PIECES = 4
RS_PIECE = ROWS // RS_PIECES
HALF = MEMBERS // 2
TALL = 192 * GROUPS
MESH = pl.DeviceIdType.MESH
F32 = jnp.float32
BF16 = jnp.bfloat16
LOSS_SCALE = 1.0 / math.sqrt(TOK * MEMBERS)
SHRINK = 1.0 / math.sqrt(D)
RANK_SCALE = 1.0 / math.sqrt(R)


PLANE = sorted(
    (
        (dy, dx, dc)
        for dy in range(SIDE)
        for dx in range(SIDE)
        for dc in range(2)
        if dy or dx or dc
    ),
    key=lambda o: (-min(o[0], SIDE - o[0]) - min(o[1], SIDE - o[1]), o),
)


def dot(a, b):
    return jnp.dot(a, b, preferred_element_type=F32)


def iota(shape, axis):
    return lax.broadcasted_iota(jnp.int32, shape, axis)


def step_kernel(
    codes_hbm,
    hyper_hbm,
    frozen_hbm,
    tokens_hbm,
    teacher_hbm,
    seq_ref,
    share_ref,
    counts_ref,
    out_ref,
    codes_ref,
    hyper_ref,
    w_buf,
    tok_buf,
    teach_buf,
    tok_blocks,
    tok_t,
    grad_buf,
    perm_buf,
    stage,
    send_small,
    recv_small,
    send_back,
    recv_back,
    ag_buf,
    tall,
    low_rows,
    b_mat,
    acc,
    own,
    send_run,
    recv_run,
    local_sem,
    small_r,
    back_r,
    out_s,
    wz_r,
    p1_r,
    p2_r,
    die_r,
    ag_r,
    rs_r,
):
    dp = lax.axis_index("dp")
    z = lax.axis_index("mp")
    c = lax.rem(dp, 2)
    x = lax.rem(dp // 2, SIDE)
    y = dp // (2 * SIDE)
    f = 1 - 2 * c

    def wrap(value, size):
        return lax.rem(value + 2 * size, size)

    def place(yy, xx):
        return (yy * SIDE + xx) * 2 + c

    def remote(src, dst, ssem, rsem, to_dp, to_z):
        return pltpu.make_async_remote_copy(
            src_ref=src,
            dst_ref=dst,
            send_sem=ssem,
            recv_sem=rsem,
            device_id=(to_dp, to_z),
            device_id_type=MESH,
        )

    small_s, back_s, wz_s, p1_s, p2_s, die_s, ag_s, rs_s = (out_s.at[i] for i in range(8))

    def send(src, dst, ssem, rsem, to_dp, to_z):
        remote(src, dst, ssem, rsem, to_dp, to_z).start()

    def arrive(dst, rsem):
        remote(dst, dst, out_s.at[0], rsem, dp, z).wait_recv()

    def all_sent(like, ssem):
        remote(like, like, ssem, small_r, dp, z).wait_send()

    local = []
    for yy in range(SIDE):
        for cc in range(2):
            local.append(
                pltpu.make_async_copy(
                    frozen_hbm.at[:, pl.ds((2 * yy + cc) * 128, 128)],
                    w_buf.at[yy, cc, pl.ds(pl.multiple_of(BLK * z, 16), BLK), :],
                    local_sem.at[0],
                )
            )
    for copy in local:
        copy.start()
    codes_copy = pltpu.make_async_copy(codes_hbm, codes_ref, local_sem.at[3])
    hyper_copy = pltpu.make_async_copy(hyper_hbm, hyper_ref, local_sem.at[4])
    codes_copy.start()
    hyper_copy.start()

    tok_copy = pltpu.make_async_copy(tokens_hbm, tok_buf, local_sem.at[1])
    teach_copy = pltpu.make_async_copy(teacher_hbm, teach_buf, local_sem.at[2])
    tok_copy.start()
    teach_copy.start()

    barrier = pltpu.get_barrier_semaphore()

    def peer(offset, sign):
        dy, dx, dc = offset
        core = c if dc == 0 else 1 - c
        return (wrap(y + sign * dy, SIDE) * SIDE + wrap(x + sign * dx, SIDE)) * 2 + core

    for offset in PLANE:
        pl.semaphore_signal(barrier, inc=1, device_id=(peer(offset, 1), z), device_id_type=MESH)

    for shift in (1, -1, 2, -2):
        pl.semaphore_signal(
            barrier, inc=1, device_id=(dp, wrap(z + shift, MEMBERS)), device_id_type=MESH
        )

    pl.semaphore_wait(barrier, GROUPS + 3)

    def w_block(way, d):
        return wrap(z - f * d if way == 0 else z + f * d, MEMBERS)

    def w_rows(start, size):
        return pl.ds(pl.multiple_of(start, 16), size)

    def w_slice(zb):
        return w_buf.at[y, c, w_rows(BLK * zb + SLICE * x, SLICE), :]

    def w_piece(way, phase, zb, i):
        if way == 0 and phase == 1:
            return w_buf.at[y, c, w_rows(BLK * zb + SLICE * i, SLICE), :]
        if way == 0:
            return w_buf.at[i, c, w_rows(BLK * zb, BLK), :]
        if phase == 1:
            return w_buf.at[i, c, w_rows(BLK * zb + SLICE * x, SLICE), :]
        return w_buf.at[:, c, w_rows(BLK * zb + SLICE * i, SLICE), :]

    def along(way, phase):
        return x if (way == 0) == (phase == 1) else y

    def shifted(way, phase, by):
        if (way == 0) == (phase == 1):
            return place(y, wrap(x + by, SIDE))
        return place(wrap(y + by, SIDE), x)

    def w_reach(way):
        return HALF if way == 0 else HALF - 1

    def z_to(way):
        return wrap(z + f if way == 0 else z - f, MEMBERS)

    def send_z(way, d):
        ref = w_slice(w_block(way, d - 1))
        send(ref, ref, wz_s, wz_r.at[way, d - 1], dp, z_to(way))

    def plane_send(way, phase, d, frm, kind, by):
        ref = w_piece(way, phase, w_block(way, d), wrap(along(way, phase) + frm, SIDE))
        if phase == 1:
            ssem, rsem = p1_s, p1_r.at[way, d - 1]
        else:
            ssem, rsem = p2_s, p2_r.at[way, d - 1, min(kind, 1)]
        send(ref, ref, ssem, rsem, shifted(way, phase, by), z)

    def twin_send(way, d, frm):
        ref = w_piece(way, 2, w_block(way, d), wrap(along(way, 2) + frm, SIDE))
        send(ref, ref, die_s, die_r.at[way, d - 1], dp + f, z)

    def twin_block(way, d):
        return wrap(z + f * d if way == 0 else z - f * d, MEMBERS)

    def twin_wait(way, d):
        arrive(
            w_buf.at[:, 1 - c, w_rows(BLK * twin_block(way, d), BLK), :], die_r.at[way, d - 1]
        )

    def take_z(way, d):
        ref = w_slice(w_block(way, d))
        arrive(ref, wz_r.at[way, d - 1])
        if d < w_reach(way):
            send_z(way, d + 1)
        plane_send(way, 1, d, 0, 0, f)
        plane_send(way, 1, d, 0, 1, -f)
        plane_send(way, 1, d, 0, 2, 2 * f)

    def start_second(way, d):
        arrive(w_buf.at[0, c, pl.ds(0, 3 * SLICE), :], p1_r.at[way, d - 1])
        plane_send(way, 2, d, 0, 0, f)
        plane_send(way, 2, d, 0, 1, -f)
        twin_send(way, d, 0)

    def relay_second(way, d):
        arrive(
            w_piece(way, 2, w_block(way, d), wrap(along(way, 2) - f, SIDE)), p2_r.at[way, d - 1, 0]
        )
        plane_send(way, 2, d, -f, 2, f)
        twin_send(way, d, -f)

    def end_second(way, d):
        arrive(w_buf.at[0, c, pl.ds(0, 2 * BLK), :], p2_r.at[way, d - 1, 1])
        twin_send(way, d, f)
        twin_send(way, d, -2 * f)

    def ag_piece(way, d, p):
        return ag_buf.at[w_block(way, d), pl.ds(p * PIECE, PIECE), :]

    def send_ag(way, d, p):
        ref = ag_piece(way, d - 1, p)
        send(ref, ref, ag_s, ag_r.at[way, d - 1, p], dp, z_to(way))

    def get_ag(way, d, p):
        arrive(ag_piece(way, d, p), ag_r.at[way, d - 1, p])
        if d < w_reach(way):
            send_ag(way, d + 1, p)

    def spread(m):
        block = jnp.concatenate(
            [ag_buf[m, pl.ds(96 * slot, 96), :] for slot in range(TPG)], axis=1
        )
        moved = dot(block, perm_buf[...])
        for s in range(3):
            for j in range(4):
                tall[pl.ds(12 * m + 4 * s + j, GROUPS, stride=192), :] = moved[
                    32 * s : 32 * (s + 1), 128 * j : 128 * (j + 1)
                ]
        for slot in range(TPG):
            for s in range(3):
                last = ag_buf[m, pl.ds(96 * slot + 32 * s + 16, 16), :].astype(F32)
                low_rows[slot, pl.ds(3 * m + s, 8, stride=48), :] = last[8:16]

    own_rows = w_buf.at[:, :, w_rows(BLK * z, BLK), :]
    pltpu.make_async_copy(own_rows, own_rows, local_sem.at[0]).wait()
    for way in (0, 1):
        send_z(way, 1)

    share = share_ref[...].astype(F32)
    g_row = lax.rem(iota((TPG * GROUPS, GROUPS), 0), GROUPS)
    g_col = iota((TPG * GROUPS, GROUPS), 1)
    share_all = jnp.broadcast_to(share, (TPG * GROUPS, GROUPS))
    first = jnp.sum(jnp.where(g_col < g_row, share_all, 0.0), axis=1, keepdims=True)
    mine = jnp.sum(jnp.where(g_col == g_row, share_all, 0.0), axis=1, keepdims=True)
    slot_row = (iota((TPG * GROUPS, TASKS), 0) // GROUPS).astype(F32)
    task_col = iota((TPG * GROUPS, TASKS), 1).astype(F32)
    picks = (task_col == first + slot_row) & (slot_row < mine)
    codes_copy.wait()
    hyper_copy.wait()
    codes_sel = dot(jnp.where(picks, 1.0, 0.0).astype(BF16), codes_ref[...]).astype(BF16)
    stage[pl.ds(ROWS, 128), :] = jnp.zeros((128, 128), F32)
    for s in range(3):
        cols = dot(codes_sel, hyper_ref[:, 128 * s : 128 * (s + 1)]).astype(BF16).astype(F32)
        for slot in range(TPG):
            stage[pl.ds((slot * 3 + s) * GROUPS, GROUPS), :] = cols[
                slot * GROUPS : (slot + 1) * GROUPS
            ]

    for g in range(GROUPS):
        send_small[g] = stage[pl.ds(g, 16, stride=GROUPS), :].astype(BF16)

    def exchange(out, into, ssem, rsem):
        for offset in PLANE:
            to = peer(offset, 1)
            send(out.at[to], into.at[dp], ssem, rsem, to, z)

    def exchanged(into, rsem):
        arrive(into.at[pl.ds(0, GROUPS - 1)], rsem)

    exchange(send_small, recv_small, small_s, small_r)

    row = iota((512, 512), 0)
    target = ((row >> 5) & 3) * 128 + (row >> 7) * 32 + (row & 31)
    perm_buf[...] = jnp.where(iota((512, 512), 1) == target, 1.0, 0.0).astype(BF16)

    ways = [(way, d) for d in range(1, HALF + 1) for way in (0, 1) if d <= w_reach(way)]

    def at(d):
        return [w for w in ways if w[1] == d]

    def add_up(cols, total):
        acc[:, cols] = acc[:, cols] + total

    def frozen(blocks, put=add_up):
        for q in range(SIDE):
            total = None
            for zb in blocks:
                rows = w_rows(BLK * zb, BLK)
                wide = jnp.concatenate([w_buf[q, 0, rows, :], w_buf[q, 1, rows, :]], axis=1)
                part = dot(tok_blocks[zb], wide)
                total = part if total is None else total + part
            put(pl.ds(256 * q, 256), total)

    def prepare(k):
        for zb in (2 * k, 2 * k + 1):
            tok_blocks[zb] = tok_buf[:, BLK * zb : BLK * (zb + 1)]
        tok_t[pl.ds(2 * BLK * k, 2 * BLK), :] = tok_buf[:, 2 * BLK * k : 2 * BLK * (k + 1)].T

    tok_copy.wait()
    teach_copy.wait()
    for k in range(MEMBERS // 2):
        prepare(k)
    acc[...] = -teach_buf[...].astype(F32)

    for way, d in at(1) + at(2):
        take_z(way, d)
    for way, d in at(1):
        start_second(way, d)

    recv_small[dp] = send_small[dp]

    exchanged(recv_small, small_r)

    stage[...] = recv_small[...].astype(F32).reshape(GROUPS * 16, 128)
    for k in range(3 * TPG):
        ag_buf[z, pl.ds(32 * k, 32), :] = stage[pl.ds(k, GROUPS, stride=16), :].astype(BF16)

    for way in (0, 1):
        for p in range(PIECES):
            send_ag(way, 1, p)
    spread(z)

    def get_piece(t, p):
        for way, d in at(t - 2):
            get_ag(way, d, p)

    def steps(t):
        for way, d in at(t):
            take_z(way, d)
        for way, d in at(t - 1):
            start_second(way, d)
        get_piece(t, 0)
        get_piece(t, 1)
        for way, d in at(t - 4):
            end_second(way, d)
        get_piece(t, 2)
        for way, d in at(t - 3):
            spread(w_block(way, d))
        get_piece(t, 3)
        for way, d in at(t - 2):
            relay_second(way, d)

    def finish(*distances):
        blocks = [wd for d in distances for wd in at(d)]
        for way, d in blocks:
            twin_wait(way, d)
        frozen([w_block(way, d) for way, d in blocks])

    steps(3)
    frozen([z])
    for t in range(4, HALF + 4):
        steps(t)
        if t == 7:
            finish(1, 2)
        if t == 9:
            finish(3, 4)

    seq0 = seq_ref[0]
    seq1 = seq_ref[1]
    upper = iota((TOK, 128), 0) < SEQ_LEN
    slot_of = jnp.where(upper, seq0, seq1)
    chosen = slot_of == iota((TOK, 128), 1) // R
    low_all = jnp.zeros((TOK, 128), F32)
    for k in range(8):
        low_all = low_all + dot(
            tok_buf[:, 640 * k : 640 * (k + 1)], tall[pl.ds(640 * k, 640), :].astype(BF16)
        )
    low = jnp.where(chosen, low_all * SHRINK, 0.0).astype(BF16)
    for slot in range(TPG):
        for k in range(8):
            b_mat[pl.ds(32 * slot, 32), 128 * k : 128 * (k + 1)] = low_rows[
                slot, pl.ds(128 + k, 32, stride=8), :
            ].astype(BF16)

    lane = iota((1, GROUPS), 1)
    own_first = jnp.sum(jnp.where(lane < dp, share, 0.0), axis=1, keepdims=True)
    counts = counts_ref[...].astype(F32)
    weights = (jnp.sum(counts, axis=1, keepdims=True) / TASKS) / counts
    task_lane = iota((1, TASKS), 1).astype(F32)

    def weight_of(slot):
        hit = task_lane == own_first + slot.astype(F32)
        return jnp.sum(jnp.where(hit, weights, 0.0), axis=1, keepdims=True) * LOSS_SCALE

    weight0 = weight_of(seq0)
    weight1 = weight_of(seq1)

    for q in range(SIDE):
        cols = pl.ds(256 * q, 256)
        acc[:, cols] = acc[:, cols] + dot(low, b_mat[:, cols]) * RANK_SCALE
    finish(5, 6)
    steps(HALF + 4)
    finish(7)

    def weigh(cols, total):
        full = acc[:, cols] + total
        grad_buf[:SEQ_LEN, cols] = (full[:SEQ_LEN] * weight0).astype(BF16)
        grad_buf[SEQ_LEN:, cols] = (full[SEQ_LEN:] * weight1).astype(BF16)

    for way, d in at(HALF):
        twin_wait(way, d)
    frozen([w_block(way, d) for way, d in at(HALF)], weigh)

    grad = grad_buf[...]
    low_grad = lax.dot_general(
        grad, b_mat[...], (((1,), (1,)), ((), ())), preferred_element_type=F32
    )
    low_grad = jnp.where(chosen, low_grad * RANK_SCALE, 0.0).astype(BF16)
    for k in range(8):
        tall[pl.ds(640 * k, 640), :] = dot(tok_t[pl.ds(640 * k, 640), :], low_grad) * SHRINK
    tall[pl.ds(D, TALL - D), :] = jnp.zeros((TALL - D, 128), F32)
    second = (
        lax.dot_general(low, grad, (((0,), (0,)), ((), ())), preferred_element_type=F32)
        * RANK_SCALE
    )
    for slot in range(TPG):
        low_rows[slot, pl.ds(0, 128), :] = jnp.zeros((128, 128), F32)
        for k in range(8):
            low_rows[slot, pl.ds(128 + k, 32, stride=8), :] = second[
                32 * slot : 32 * (slot + 1), 128 * k : 128 * (k + 1)
            ]

    def collect(m):
        parts = [
            jnp.concatenate(
                [
                    tall[pl.ds(12 * m + 4 * s + j, GROUPS, stride=192), :].astype(BF16)
                    for j in range(4)
                ],
                axis=1,
            )
            for s in range(3)
        ]
        moved = dot(jnp.concatenate(parts, axis=0), perm_buf[...])
        for slot in range(TPG):
            for s in range(3):
                from_a = moved[32 * s : 32 * (s + 1), 128 * slot : 128 * (slot + 1)]
                from_b = low_rows[slot, pl.ds(3 * m + s, 8, stride=48), :]
                flat = 48 * (iota((8, 128), 0) + 24) + 3 * m + s
                tail = jnp.where(flat >= D * R // 128, from_b, from_a[24:])
                own[m, pl.ds(96 * slot + 32 * s, 32), :] = jnp.concatenate(
                    [from_a[:24], tail], axis=0
                ).astype(BF16)

    def rs_dest(way, k):
        return wrap(z + f * (HALF - k) if way == 0 else z - f * (HALF - 1 - k), MEMBERS)

    def run_send(way, k, p, src):
        far = wrap(z + 2 * f if way == 0 else z - 2 * f, MEMBERS)
        send(
            src,
            recv_run.at[way, k, pl.ds(p * RS_PIECE, RS_PIECE), :],
            rs_s,
            rs_r.at[way, k, p],
            dp,
            far if k == 0 else z_to(way),
        )

    for k in (0, 1):
        for way in (0, 1):
            m = rs_dest(way, k)
            collect(m)
            for p in range(RS_PIECES):
                run_send(way, k, p, own.at[m, pl.ds(p * RS_PIECE, RS_PIECE), :])
    for k in range(2, HALF):
        live = [way for way in (0, 1) if k < w_reach(way)]
        for way in live:
            collect(rs_dest(way, k))
        for p in range(RS_PIECES):
            rows = pl.ds(p * RS_PIECE, RS_PIECE)
            for way in live:
                arrive(recv_run.at[way, k - 1, rows, :], rs_r.at[way, k - 1, p])
                total = recv_run[way, k - 1, rows, :].astype(F32) + own[
                    rs_dest(way, k), rows, :
                ].astype(F32)
                if k == 2:
                    arrive(recv_run.at[way, 0, rows, :], rs_r.at[way, 0, p])
                    total = total + recv_run[way, 0, rows, :].astype(F32)
                send_run[way, k, rows, :] = total.astype(BF16)
                run_send(way, k, p, send_run.at[way, k, rows, :])
    collect(z)
    for p in range(RS_PIECES):
        rows = pl.ds(p * RS_PIECE, RS_PIECE)
        for way in (0, 1):
            k = w_reach(way) - 1
            arrive(recv_run.at[way, k, rows, :], rs_r.at[way, k, p])
        stage[rows, :] = (
            recv_run[0, HALF - 1, rows, :].astype(F32)
            + recv_run[1, HALF - 2, rows, :].astype(F32)
            + own[z, rows, :].astype(F32)
        )
    stage[pl.ds(ROWS, 128), :] = jnp.zeros((128, 128), F32)

    for g in range(GROUPS):
        send_back[g] = stage[pl.ds(g, 16, stride=GROUPS), :].astype(BF16)

    exchange(send_back, recv_back, back_s, back_r)
    all_sent(send_small.at[pl.ds(0, GROUPS - 1)], small_s)
    all_sent(w_buf.at[0, 0, pl.ds(0, 15 * SLICE), :], wz_s)
    all_sent(w_buf.at[0, 0, pl.ds(0, 45 * SLICE), :], p1_s)
    all_sent(w_buf.at[:, 0, pl.ds(0, 45 * SLICE), :], p2_s)
    all_sent(w_buf.at[:, 0, pl.ds(0, 60 * SLICE), :], die_s)
    all_sent(ag_buf.at[pl.ds(0, 15)], ag_s)
    all_sent(own.at[pl.ds(0, 15)], rs_s)

    recv_back[dp] = send_back[dp]
    exchanged(recv_back, back_r)

    stage[...] = recv_back[...].astype(F32).reshape(GROUPS * 16, 128)
    for s in range(3):
        sums = jnp.concatenate(
            [stage[pl.ds(slot * 3 + s, GROUPS, stride=16), :] for slot in range(TPG)], axis=0
        ).astype(BF16)
        out_ref[:, 128 * s : 128 * (s + 1)] = lax.dot_general(
            codes_sel, sums, (((0,), (0,)), ((), ())), preferred_element_type=F32
        )

    all_sent(send_back.at[pl.ds(0, GROUPS - 1)], back_s)


def shards(
    task_codes, hyper_weight, frozen_weight, tokens, teacher, seq_slot, task_share, token_counts
):
    vmem = pl.BlockSpec(memory_space=pltpu.VMEM)
    smem = pl.BlockSpec(memory_space=pltpu.SMEM)
    hbm = pl.BlockSpec(memory_space=pl.ANY)
    dma = pltpu.SemaphoreType.DMA
    small = pltpu.VMEM((GROUPS, 16, 128), BF16)
    return pl.pallas_call(
        step_kernel,
        out_shape=jax.ShapeDtypeStruct((128, 384), F32),
        in_specs=[hbm, hbm, hbm, hbm, hbm, smem, vmem, vmem],
        out_specs=vmem,
        scratch_shapes=[
            pltpu.VMEM((TASKS, 128), BF16),
            pltpu.VMEM((128, 384), BF16),
            pltpu.VMEM((SIDE, 2, D, 128), BF16),
            pltpu.VMEM((TOK, D), BF16),
            pltpu.VMEM((TOK, KV), BF16),
            pltpu.VMEM((MEMBERS, TOK, BLK), BF16),
            pltpu.VMEM((D, TOK), BF16),
            pltpu.VMEM((TOK, KV), BF16),
            pltpu.VMEM((512, 512), BF16),
            pltpu.VMEM((512, 128), F32),
            small,
            small,
            small,
            small,
            pltpu.VMEM((MEMBERS, ROWS, 128), BF16),
            pltpu.VMEM((TALL, 128), F32),
            pltpu.VMEM((TPG, ROWS, 128), F32),
            pltpu.VMEM((128, KV), BF16),
            pltpu.VMEM((TOK, KV), F32),
            pltpu.VMEM((MEMBERS, ROWS, 128), BF16),
            pltpu.VMEM((2, HALF, ROWS, 128), BF16),
            pltpu.VMEM((2, HALF, ROWS, 128), BF16),
            dma((5,)),
            dma,
            dma,
            dma((8,)),
            dma((2, HALF)),
            dma((2, HALF)),
            dma((2, HALF, 2)),
            dma((2, HALF)),
            dma((2, HALF, PIECES)),
            dma((2, HALF, RS_PIECES)),
        ],
        compiler_params=pltpu.CompilerParams(collective_id=0, has_side_effects=True),
    )(
        task_codes,
        hyper_weight,
        frozen_weight,
        tokens,
        teacher,
        seq_slot,
        task_share.reshape(1, -1),
        token_counts.reshape(1, -1),
    )


def solution(mesh):
    placed = (
        P(),
        P(None, ("dp", "mp")),
        P("mp", None),
        P(("dp", "mp"), None),
        P(("dp", "mp"), None),
        P(("dp", "mp")),
        P(),
        P(),
    )
    return jax.shard_map(
        shards, mesh=mesh, in_specs=placed, out_specs=P(None, ("dp", "mp")), check_vma=False
    )
```

```python
import math

import jax
import jax.numpy as jnp
from jax import lax
from jax.experimental import pallas as pl
from jax.experimental.pallas import tpu as pltpu
from jax.sharding import PartitionSpec as P

D = 5120
KV = 1024
R = 32
TPG = 4
SEQ_LEN = 128
GROUPS = 32
MEMBERS = 16
SIDE = 4
TASKS = 64
TOK = 256
BLK = D // MEMBERS
SLICE = BLK // SIDE
ROWS = 3 * TPG * GROUPS
PIECES = 4
PIECE = ROWS // PIECES
RS_PIECES = 4
RS_PIECE = ROWS // RS_PIECES
HALF = MEMBERS // 2
TALL = 192 * GROUPS
MESH = pl.DeviceIdType.MESH
F32 = jnp.float32
BF16 = jnp.bfloat16
LOSS_SCALE = 1.0 / math.sqrt(TOK * MEMBERS)
SHRINK = 1.0 / math.sqrt(D)
RANK_SCALE = 1.0 / math.sqrt(R)


PLANE = sorted(
    (
        (dy, dx, dc)
        for dy in range(SIDE)
        for dx in range(SIDE)
        for dc in range(2)
        if dy or dx or dc
    ),
    key=lambda o: (-min(o[0], SIDE - o[0]) - min(o[1], SIDE - o[1]), o),
)


def dot(a, b):
    return jnp.dot(a, b, preferred_element_type=F32)


def iota(shape, axis):
    return lax.broadcasted_iota(jnp.int32, shape, axis)


def step_kernel(
    codes_hbm,
    hyper_hbm,
    frozen_hbm,
    tokens_hbm,
    teacher_hbm,
    seq_ref,
    share_ref,
    counts_ref,
    out_ref,
    codes_ref,
    hyper_ref,
    w_buf,
    tok_buf,
    teach_buf,
    tok_blocks,
    tok_t,
    grad_buf,
    perm_buf,
    stage,
    send_small,
    recv_small,
    send_back,
    recv_back,
    ag_buf,
    tall,
    low_rows,
    b_mat,
    acc,
    own,
    send_run,
    recv_run,
    local_sem,
    small_r,
    back_r,
    out_s,
    wz_r,
    p1_r,
    p2_r,
    die_r,
    ag_r,
    rs_r,
):
    dp = lax.axis_index("dp")
    z = lax.axis_index("mp")
    c = lax.rem(dp, 2)
    x = lax.rem(dp // 2, SIDE)
    y = dp // (2 * SIDE)
    f = 1 - 2 * c

    def wrap(value, size):
        return lax.rem(value + 2 * size, size)

    def place(yy, xx):
        return (yy * SIDE + xx) * 2 + c

    def remote(src, dst, ssem, rsem, to_dp, to_z):
        return pltpu.make_async_remote_copy(
            src_ref=src,
            dst_ref=dst,
            send_sem=ssem,
            recv_sem=rsem,
            device_id=(to_dp, to_z),
            device_id_type=MESH,
        )

    small_s, back_s, wz_s, p1_s, p2_s, die_s, ag_s, rs_s = (out_s.at[i] for i in range(8))

    def send(src, dst, ssem, rsem, to_dp, to_z):
        remote(src, dst, ssem, rsem, to_dp, to_z).start()

    def arrive(dst, rsem):
        remote(dst, dst, out_s.at[0], rsem, dp, z).wait_recv()

    def all_sent(like, ssem):
        remote(like, like, ssem, small_r, dp, z).wait_send()

    local = []
    for yy in range(SIDE):
        for cc in range(2):
            local.append(
                pltpu.make_async_copy(
                    frozen_hbm.at[:, pl.ds((2 * yy + cc) * 128, 128)],
                    w_buf.at[yy, cc, pl.ds(pl.multiple_of(BLK * z, 16), BLK), :],
                    local_sem.at[0],
                )
            )
    for copy in local:
        copy.start()
    codes_copy = pltpu.make_async_copy(codes_hbm, codes_ref, local_sem.at[3])
    hyper_copy = pltpu.make_async_copy(hyper_hbm, hyper_ref, local_sem.at[4])
    codes_copy.start()
    hyper_copy.start()

    tok_copy = pltpu.make_async_copy(tokens_hbm, tok_buf, local_sem.at[1])
    teach_copy = pltpu.make_async_copy(teacher_hbm, teach_buf, local_sem.at[2])
    tok_copy.start()
    teach_copy.start()

    barrier = pltpu.get_barrier_semaphore()

    def peer(offset, sign):
        dy, dx, dc = offset
        core = c if dc == 0 else 1 - c
        return (wrap(y + sign * dy, SIDE) * SIDE + wrap(x + sign * dx, SIDE)) * 2 + core

    for offset in PLANE:
        pl.semaphore_signal(barrier, inc=1, device_id=(peer(offset, 1), z), device_id_type=MESH)

    for shift in (1, -1, 2, -2):
        pl.semaphore_signal(
            barrier, inc=1, device_id=(dp, wrap(z + shift, MEMBERS)), device_id_type=MESH
        )

    pl.semaphore_wait(barrier, GROUPS + 3)

    def w_block(way, d):
        return wrap(z - f * d if way == 0 else z + f * d, MEMBERS)

    def w_rows(start, size):
        return pl.ds(pl.multiple_of(start, 16), size)

    def w_slice(zb):
        return w_buf.at[y, c, w_rows(BLK * zb + SLICE * x, SLICE), :]

    def w_piece(way, phase, zb, i):
        if way == 0 and phase == 1:
            return w_buf.at[y, c, w_rows(BLK * zb + SLICE * i, SLICE), :]
        if way == 0:
            return w_buf.at[i, c, w_rows(BLK * zb, BLK), :]
        if phase == 1:
            return w_buf.at[i, c, w_rows(BLK * zb + SLICE * x, SLICE), :]
        return w_buf.at[:, c, w_rows(BLK * zb + SLICE * i, SLICE), :]

    def along(way, phase):
        return x if (way == 0) == (phase == 1) else y

    def shifted(way, phase, by):
        if (way == 0) == (phase == 1):
            return place(y, wrap(x + by, SIDE))
        return place(wrap(y + by, SIDE), x)

    def w_reach(way):
        return HALF if way == 0 else HALF - 1

    def z_to(way):
        return wrap(z + f if way == 0 else z - f, MEMBERS)

    def send_z(way, d):
        ref = w_slice(w_block(way, d - 1))
        send(ref, ref, wz_s, wz_r.at[way, d - 1], dp, z_to(way))

    def plane_send(way, phase, d, frm, kind, by):
        ref = w_piece(way, phase, w_block(way, d), wrap(along(way, phase) + frm, SIDE))
        if phase == 1:
            ssem, rsem = p1_s, p1_r.at[way, d - 1]
        else:
            ssem, rsem = p2_s, p2_r.at[way, d - 1, min(kind, 1)]
        send(ref, ref, ssem, rsem, shifted(way, phase, by), z)

    def twin_send(way, d, frm):
        ref = w_piece(way, 2, w_block(way, d), wrap(along(way, 2) + frm, SIDE))
        send(ref, ref, die_s, die_r.at[way, d - 1], dp + f, z)

    def twin_block(way, d):
        return wrap(z + f * d if way == 0 else z - f * d, MEMBERS)

    def twin_wait(way, d):
        arrive(
            w_buf.at[:, 1 - c, w_rows(BLK * twin_block(way, d), BLK), :], die_r.at[way, d - 1]
        )

    def take_z(way, d):
        ref = w_slice(w_block(way, d))
        arrive(ref, wz_r.at[way, d - 1])
        if d < w_reach(way):
            send_z(way, d + 1)
        plane_send(way, 1, d, 0, 0, f)
        plane_send(way, 1, d, 0, 1, -f)
        plane_send(way, 1, d, 0, 2, 2 * f)

    def start_second(way, d):
        arrive(w_buf.at[0, c, pl.ds(0, 3 * SLICE), :], p1_r.at[way, d - 1])
        plane_send(way, 2, d, 0, 0, f)
        plane_send(way, 2, d, 0, 1, -f)
        twin_send(way, d, 0)

    def relay_second(way, d):
        arrive(
            w_piece(way, 2, w_block(way, d), wrap(along(way, 2) - f, SIDE)), p2_r.at[way, d - 1, 0]
        )
        plane_send(way, 2, d, -f, 2, f)
        twin_send(way, d, -f)

    def end_second(way, d):
        arrive(w_buf.at[0, c, pl.ds(0, 2 * BLK), :], p2_r.at[way, d - 1, 1])
        twin_send(way, d, f)
        twin_send(way, d, -2 * f)

    def ag_piece(way, d, p):
        return ag_buf.at[w_block(way, d), pl.ds(p * PIECE, PIECE), :]

    def send_ag(way, d, p):
        ref = ag_piece(way, d - 1, p)
        send(ref, ref, ag_s, ag_r.at[way, d - 1, p], dp, z_to(way))

    def get_ag(way, d, p):
        arrive(ag_piece(way, d, p), ag_r.at[way, d - 1, p])
        if d < w_reach(way):
            send_ag(way, d + 1, p)

    def spread(m):
        block = jnp.concatenate(
            [ag_buf[m, pl.ds(96 * slot, 96), :] for slot in range(TPG)], axis=1
        )
        moved = dot(block, perm_buf[...])
        for s in range(3):
            for j in range(4):
                tall[pl.ds(12 * m + 4 * s + j, GROUPS, stride=192), :] = moved[
                    32 * s : 32 * (s + 1), 128 * j : 128 * (j + 1)
                ]
        for slot in range(TPG):
            for s in range(3):
                last = ag_buf[m, pl.ds(96 * slot + 32 * s + 16, 16), :].astype(F32)
                low_rows[slot, pl.ds(3 * m + s, 8, stride=48), :] = last[8:16]

    own_rows = w_buf.at[:, :, w_rows(BLK * z, BLK), :]
    pltpu.make_async_copy(own_rows, own_rows, local_sem.at[0]).wait()
    for way in (0, 1):
        send_z(way, 1)

    share = share_ref[...].astype(F32)
    g_row = lax.rem(iota((TPG * GROUPS, GROUPS), 0), GROUPS)
    g_col = iota((TPG * GROUPS, GROUPS), 1)
    share_all = jnp.broadcast_to(share, (TPG * GROUPS, GROUPS))
    first = jnp.sum(jnp.where(g_col < g_row, share_all, 0.0), axis=1, keepdims=True)
    mine = jnp.sum(jnp.where(g_col == g_row, share_all, 0.0), axis=1, keepdims=True)
    slot_row = (iota((TPG * GROUPS, TASKS), 0) // GROUPS).astype(F32)
    task_col = iota((TPG * GROUPS, TASKS), 1).astype(F32)
    picks = (task_col == first + slot_row) & (slot_row < mine)
    codes_copy.wait()
    hyper_copy.wait()
    codes_sel = dot(jnp.where(picks, 1.0, 0.0).astype(BF16), codes_ref[...]).astype(BF16)
    stage[pl.ds(ROWS, 128), :] = jnp.zeros((128, 128), F32)
    for s in range(3):
        cols = dot(codes_sel, hyper_ref[:, 128 * s : 128 * (s + 1)]).astype(BF16).astype(F32)
        for slot in range(TPG):
            stage[pl.ds((slot * 3 + s) * GROUPS, GROUPS), :] = cols[
                slot * GROUPS : (slot + 1) * GROUPS
            ]

    for g in range(GROUPS):
        send_small[g] = stage[pl.ds(g, 16, stride=GROUPS), :].astype(BF16)

    def exchange(out, into, ssem, rsem):
        for offset in PLANE:
            to = peer(offset, 1)
            send(out.at[to], into.at[dp], ssem, rsem, to, z)

    def exchanged(into, rsem):
        arrive(into.at[pl.ds(0, GROUPS - 1)], rsem)

    exchange(send_small, recv_small, small_s, small_r)

    row = iota((512, 512), 0)
    target = ((row >> 5) & 3) * 128 + (row >> 7) * 32 + (row & 31)
    perm_buf[...] = jnp.where(iota((512, 512), 1) == target, 1.0, 0.0).astype(BF16)

    ways = [(way, d) for d in range(1, HALF + 1) for way in (0, 1) if d <= w_reach(way)]

    def at(d):
        return [w for w in ways if w[1] == d]

    def add_up(cols, total):
        acc[:, cols] = acc[:, cols] + total

    def frozen(blocks, put=add_up):
        for q in range(SIDE):
            total = None
            for zb in blocks:
                rows = w_rows(BLK * zb, BLK)
                wide = jnp.concatenate([w_buf[q, 0, rows, :], w_buf[q, 1, rows, :]], axis=1)
                part = dot(tok_blocks[zb], wide)
                total = part if total is None else total + part
            put(pl.ds(256 * q, 256), total)

    def prepare(k):
        for zb in (2 * k, 2 * k + 1):
            tok_blocks[zb] = tok_buf[:, BLK * zb : BLK * (zb + 1)]
        tok_t[pl.ds(2 * BLK * k, 2 * BLK), :] = tok_buf[:, 2 * BLK * k : 2 * BLK * (k + 1)].T

    for way, d in at(1):
        take_z(way, d)

    tok_copy.wait()
    teach_copy.wait()
    for k in range(MEMBERS // 2):
        prepare(k)
    acc[...] = -teach_buf[...].astype(F32)

    for way, d in at(2):
        take_z(way, d)
    for way, d in at(1):
        start_second(way, d)

    recv_small[dp] = send_small[dp]

    exchanged(recv_small, small_r)

    stage[...] = recv_small[...].astype(F32).reshape(GROUPS * 16, 128)
    for k in range(3 * TPG):
        ag_buf[z, pl.ds(32 * k, 32), :] = stage[pl.ds(k, GROUPS, stride=16), :].astype(BF16)

    for way in (0, 1):
        for p in range(PIECES):
            send_ag(way, 1, p)
    spread(z)

    def get_piece(t, p):
        for way, d in at(t - 2):
            get_ag(way, d, p)

    def steps(t):
        for way, d in at(t):
            take_z(way, d)
        for way, d in at(t - 1):
            start_second(way, d)
        get_piece(t, 0)
        get_piece(t, 1)
        for way, d in at(t - 4):
            end_second(way, d)
        get_piece(t, 2)
        for way, d in at(t - 3):
            spread(w_block(way, d))
        get_piece(t, 3)
        for way, d in at(t - 2):
            relay_second(way, d)

    def finish(*distances):
        blocks = [wd for d in distances for wd in at(d)]
        for way, d in blocks:
            twin_wait(way, d)
        frozen([w_block(way, d) for way, d in blocks])

    steps(3)
    frozen([z])
    for t in range(4, HALF + 4):
        steps(t)
        if t == 7:
            finish(1, 2)
        if t == 9:
            finish(3, 4)

    seq0 = seq_ref[0]
    seq1 = seq_ref[1]
    upper = iota((TOK, 128), 0) < SEQ_LEN
    slot_of = jnp.where(upper, seq0, seq1)
    chosen = slot_of == iota((TOK, 128), 1) // R
    low_all = jnp.zeros((TOK, 128), F32)
    for k in range(8):
        low_all = low_all + dot(
            tok_buf[:, 640 * k : 640 * (k + 1)], tall[pl.ds(640 * k, 640), :].astype(BF16)
        )
    low = jnp.where(chosen, low_all * SHRINK, 0.0).astype(BF16)
    for slot in range(TPG):
        for k in range(8):
            b_mat[pl.ds(32 * slot, 32), 128 * k : 128 * (k + 1)] = low_rows[
                slot, pl.ds(128 + k, 32, stride=8), :
            ].astype(BF16)

    lane = iota((1, GROUPS), 1)
    own_first = jnp.sum(jnp.where(lane < dp, share, 0.0), axis=1, keepdims=True)
    counts = counts_ref[...].astype(F32)
    weights = (jnp.sum(counts, axis=1, keepdims=True) / TASKS) / counts
    task_lane = iota((1, TASKS), 1).astype(F32)

    def weight_of(slot):
        hit = task_lane == own_first + slot.astype(F32)
        return jnp.sum(jnp.where(hit, weights, 0.0), axis=1, keepdims=True) * LOSS_SCALE

    weight0 = weight_of(seq0)
    weight1 = weight_of(seq1)

    for q in range(SIDE):
        cols = pl.ds(256 * q, 256)
        acc[:, cols] = acc[:, cols] + dot(low, b_mat[:, cols]) * RANK_SCALE
    finish(5, 6)
    steps(HALF + 4)
    finish(7)

    def weigh(cols, total):
        full = acc[:, cols] + total
        grad_buf[:SEQ_LEN, cols] = (full[:SEQ_LEN] * weight0).astype(BF16)
        grad_buf[SEQ_LEN:, cols] = (full[SEQ_LEN:] * weight1).astype(BF16)

    for way, d in at(HALF):
        twin_wait(way, d)
    frozen([w_block(way, d) for way, d in at(HALF)], weigh)

    grad = grad_buf[...]
    low_grad = lax.dot_general(
        grad, b_mat[...], (((1,), (1,)), ((), ())), preferred_element_type=F32
    )
    low_grad = jnp.where(chosen, low_grad * RANK_SCALE, 0.0).astype(BF16)
    for k in range(8):
        tall[pl.ds(640 * k, 640), :] = dot(tok_t[pl.ds(640 * k, 640), :], low_grad) * SHRINK
    tall[pl.ds(D, TALL - D), :] = jnp.zeros((TALL - D, 128), F32)
    second = (
        lax.dot_general(low, grad, (((0,), (0,)), ((), ())), preferred_element_type=F32)
        * RANK_SCALE
    )
    for slot in range(TPG):
        low_rows[slot, pl.ds(0, 128), :] = jnp.zeros((128, 128), F32)
        for k in range(8):
            low_rows[slot, pl.ds(128 + k, 32, stride=8), :] = second[
                32 * slot : 32 * (slot + 1), 128 * k : 128 * (k + 1)
            ]

    def collect(m):
        parts = [
            jnp.concatenate(
                [
                    tall[pl.ds(12 * m + 4 * s + j, GROUPS, stride=192), :].astype(BF16)
                    for j in range(4)
                ],
                axis=1,
            )
            for s in range(3)
        ]
        moved = dot(jnp.concatenate(parts, axis=0), perm_buf[...])
        for slot in range(TPG):
            for s in range(3):
                from_a = moved[32 * s : 32 * (s + 1), 128 * slot : 128 * (slot + 1)]
                from_b = low_rows[slot, pl.ds(3 * m + s, 8, stride=48), :]
                flat = 48 * (iota((8, 128), 0) + 24) + 3 * m + s
                tail = jnp.where(flat >= D * R // 128, from_b, from_a[24:])
                own[m, pl.ds(96 * slot + 32 * s, 32), :] = jnp.concatenate(
                    [from_a[:24], tail], axis=0
                ).astype(BF16)

    def rs_dest(way, k):
        return wrap(z + f * (HALF - k) if way == 0 else z - f * (HALF - 1 - k), MEMBERS)

    def run_send(way, k, p, src):
        far = wrap(z + 2 * f if way == 0 else z - 2 * f, MEMBERS)
        send(
            src,
            recv_run.at[way, k, pl.ds(p * RS_PIECE, RS_PIECE), :],
            rs_s,
            rs_r.at[way, k, p],
            dp,
            far if k == 0 else z_to(way),
        )

    for k in (0, 1):
        for way in (0, 1):
            m = rs_dest(way, k)
            collect(m)
            for p in range(RS_PIECES):
                run_send(way, k, p, own.at[m, pl.ds(p * RS_PIECE, RS_PIECE), :])
    for k in range(2, HALF):
        live = [way for way in (0, 1) if k < w_reach(way)]
        for way in live:
            collect(rs_dest(way, k))
        for p in range(RS_PIECES):
            rows = pl.ds(p * RS_PIECE, RS_PIECE)
            for way in live:
                arrive(recv_run.at[way, k - 1, rows, :], rs_r.at[way, k - 1, p])
                total = recv_run[way, k - 1, rows, :].astype(F32) + own[
                    rs_dest(way, k), rows, :
                ].astype(F32)
                if k == 2:
                    arrive(recv_run.at[way, 0, rows, :], rs_r.at[way, 0, p])
                    total = total + recv_run[way, 0, rows, :].astype(F32)
                send_run[way, k, rows, :] = total.astype(BF16)
                run_send(way, k, p, send_run.at[way, k, rows, :])
    collect(z)
    for p in range(RS_PIECES):
        rows = pl.ds(p * RS_PIECE, RS_PIECE)
        for way in (0, 1):
            k = w_reach(way) - 1
            arrive(recv_run.at[way, k, rows, :], rs_r.at[way, k, p])
        stage[rows, :] = (
            recv_run[0, HALF - 1, rows, :].astype(F32)
            + recv_run[1, HALF - 2, rows, :].astype(F32)
            + own[z, rows, :].astype(F32)
        )
    stage[pl.ds(ROWS, 128), :] = jnp.zeros((128, 128), F32)

    for g in range(GROUPS):
        send_back[g] = stage[pl.ds(g, 16, stride=GROUPS), :].astype(BF16)

    exchange(send_back, recv_back, back_s, back_r)
    all_sent(send_small.at[pl.ds(0, GROUPS - 1)], small_s)
    all_sent(w_buf.at[0, 0, pl.ds(0, 15 * SLICE), :], wz_s)
    all_sent(w_buf.at[0, 0, pl.ds(0, 45 * SLICE), :], p1_s)
    all_sent(w_buf.at[:, 0, pl.ds(0, 45 * SLICE), :], p2_s)
    all_sent(w_buf.at[:, 0, pl.ds(0, 60 * SLICE), :], die_s)
    all_sent(ag_buf.at[pl.ds(0, 15)], ag_s)
    all_sent(own.at[pl.ds(0, 15)], rs_s)

    recv_back[dp] = send_back[dp]
    exchanged(recv_back, back_r)

    stage[...] = recv_back[...].astype(F32).reshape(GROUPS * 16, 128)
    for s in range(3):
        sums = jnp.concatenate(
            [stage[pl.ds(slot * 3 + s, GROUPS, stride=16), :] for slot in range(TPG)], axis=0
        ).astype(BF16)
        out_ref[:, 128 * s : 128 * (s + 1)] = lax.dot_general(
            codes_sel, sums, (((0,), (0,)), ((), ())), preferred_element_type=F32
        )

    all_sent(send_back.at[pl.ds(0, GROUPS - 1)], back_s)


def shards(
    task_codes, hyper_weight, frozen_weight, tokens, teacher, seq_slot, task_share, token_counts
):
    vmem = pl.BlockSpec(memory_space=pltpu.VMEM)
    smem = pl.BlockSpec(memory_space=pltpu.SMEM)
    hbm = pl.BlockSpec(memory_space=pl.ANY)
    dma = pltpu.SemaphoreType.DMA
    small = pltpu.VMEM((GROUPS, 16, 128), BF16)
    return pl.pallas_call(
        step_kernel,
        out_shape=jax.ShapeDtypeStruct((128, 384), F32),
        in_specs=[hbm, hbm, hbm, hbm, hbm, smem, vmem, vmem],
        out_specs=vmem,
        scratch_shapes=[
            pltpu.VMEM((TASKS, 128), BF16),
            pltpu.VMEM((128, 384), BF16),
            pltpu.VMEM((SIDE, 2, D, 128), BF16),
            pltpu.VMEM((TOK, D), BF16),
            pltpu.VMEM((TOK, KV), BF16),
            pltpu.VMEM((MEMBERS, TOK, BLK), BF16),
            pltpu.VMEM((D, TOK), BF16),
            pltpu.VMEM((TOK, KV), BF16),
            pltpu.VMEM((512, 512), BF16),
            pltpu.VMEM((512, 128), F32),
            small,
            small,
            small,
            small,
            pltpu.VMEM((MEMBERS, ROWS, 128), BF16),
            pltpu.VMEM((TALL, 128), F32),
            pltpu.VMEM((TPG, ROWS, 128), F32),
            pltpu.VMEM((128, KV), BF16),
            pltpu.VMEM((TOK, KV), F32),
            pltpu.VMEM((MEMBERS, ROWS, 128), BF16),
            pltpu.VMEM((2, HALF, ROWS, 128), BF16),
            pltpu.VMEM((2, HALF, ROWS, 128), BF16),
            dma((5,)),
            dma,
            dma,
            dma((8,)),
            dma((2, HALF)),
            dma((2, HALF)),
            dma((2, HALF, 2)),
            dma((2, HALF)),
            dma((2, HALF, PIECES)),
            dma((2, HALF, RS_PIECES)),
        ],
        compiler_params=pltpu.CompilerParams(collective_id=0, has_side_effects=True),
    )(
        task_codes,
        hyper_weight,
        frozen_weight,
        tokens,
        teacher,
        seq_slot,
        task_share.reshape(1, -1),
        token_counts.reshape(1, -1),
    )


def solution(mesh):
    placed = (
        P(),
        P(None, ("dp", "mp")),
        P("mp", None),
        P(("dp", "mp"), None),
        P(("dp", "mp"), None),
        P(("dp", "mp")),
        P(),
        P(),
    )
    return jax.shard_map(
        shards, mesh=mesh, in_specs=placed, out_specs=P(None, ("dp", "mp")), check_vma=False
    )
```
